128 devices in a mesh: mp: 2 (over x_hi), gx: 8 (over z, x_lo), gy: 8 (over y, core).
Axes of the slice: x: 4 (x_hi: 2, x_lo: 2; x = x_hi * 2 + x_lo), y: 4, z: 4, core: 2. Of those that a mesh axis runs over, the one named last changes fastest.
Arguments:
- spectrum: float32 [1152, 16384], P(None, ('mp', 'gx', 'gy')), may hold values from 0.25 to 4
- source_weights: bfloat16 [4, 1152, 1152], replicated, may hold values from -0.1875 to 0.1875
- drift_weights: bfloat16 [64, 1152], replicated, may hold values from -0.1875 to 0.1875
- courant: float32 [2, 1152], replicated, may hold values from -0.45 to 0.45
- point_tile: int32 [16384, 1], P(('mp', 'gx', 'gy')), may hold values from 0 to 127; in each aligned block of 128 rows (0 to 127, 128 to 255, ...) at most 2 rows name the same one
- point_cell: int32 [16384], P(('mp', 'gx', 'gy')), may hold values from 0 to 16383
- wave_land: int32 [16384], P(('mp', 'gx', 'gy')), may hold values 0 or 1
- ocean_vel: float32 [2, 32, 2048, 1024], P(None, None, ('mp', 'gx'), 'gy'), may hold values from -6 to 6
- ocean_land: int32 [2048, 1024], P(('mp', 'gx'), 'gy'), may hold values 0 or 1
Outputs:
- energy: float32 [1152, 16384], P(None, ('mp', 'gx', 'gy'))
- ocean_out: float32 [2, 32, 2048, 1024], P(None, None, ('mp', 'gx'), 'gy')
The draws below stay inside these ranges and needn't reach their ends.
Inputs may be any that keep to these rules, and one draw needn't show every extreme that they name: `point_tile`: of the points of one device, at most 2 share one tile, and some tile receives exactly 2 of them.
All inputs are finite; a program needn't handle non-finite values. No bound on the sum of `wave_land` or of `ocean_land` on one device may be relied on, other than what follows from the above.
Results may differ from the reference program's by a relative error of at most 0.00071.
Values sent between devices are 32-bit elements; how exact they have to be, the bound alone decides.
A program may use at most 128 MiB of HBM per device.

```python
import math
import jax
import jax.numpy as jnp
import numpy as np
from jax import lax

K = 1152
LEV = 32
PBX = 4
PBY = 32
OX = 128
OY = 128
NSTEP = 2
PT_DEV = 128
P_SIZE = 16384
CAP = 2
NOX = 2048
NOY = 1024
N_MP = 2
N_GX = 8
N_GY = 8
DEVICES = 128


def touch_ends(result, key, least, largest):
    longest = result.shape.index(max(result.shape))
    spots = []
    for shift in (0, 1):
        where = [jax.random.randint(jax.random.fold_in(key, axis), (), 0, length) for axis, length in enumerate(result.shape)]
        where[longest] = (where[longest] + shift) % result.shape[longest]
        spots.append(tuple(where))
    return result.at[spots[0]].set(least).at[spots[1]].set(largest)


def steps_of(key, dims, shards, least, top_value):
    gain, own = 1.0, jax.random.fold_in(key, 6)
    for dim, blocks in shards:
        draws = jnp.exp(jax.random.uniform(jax.random.fold_in(own, dim), (blocks,), jnp.float32, least / len(shards), top_value / len(shards)))
        gain = gain * jnp.repeat(draws, dims[dim] // blocks).reshape([-1 if axis == dim else 1 for axis in range(len(dims))])
    return gain


def shared_out(key, own, number, rows, number_of, top, most, slope):
    ranking = jax.random.permutation(key, number_of)
    heavy_load, usual = load_shares(number_of, rows * top, most, slope, True), load_shares(number_of, rows * top, most, slope, False)
    places = jnp.arange(number_of)

    def named(lengths, offset_by):
        used = int((lengths > 0).sum())
        fixed = max(1, used // 4)
        shifted = fixed + (places - fixed + offset_by * (used - fixed)) % max(1, number_of - fixed)
        return jnp.zeros((number_of,), jnp.int32).at[ranking[jnp.where(places < fixed, places, shifted)]].set(jnp.asarray(lengths, jnp.int32))

    lengths = jnp.where(number % 4 == 0, named(heavy_load, number // 4), named(usual, number - number // 4 - 1))
    mixed = jax.random.permutation(jax.random.fold_in(own, 3), number_of)
    source_of, taker = mixed[0:number_of // 2 * 2:2], mixed[1:number_of // 2 * 2:2]
    margin = jnp.minimum(lengths[source_of] - 1, most - lengths[taker]) // 2
    margin = jnp.where((source_of == ranking[0]) | (taker == ranking[0]) | (lengths[taker] == 0), 0, jnp.maximum(margin, 0))
    shifted = jax.random.randint(jax.random.fold_in(own, 4), (number_of // 2,), 0, 1 << 20) % (margin + 1)
    lengths = lengths.at[source_of].add(-shifted).at[taker].add(shifted)
    labels = jnp.searchsorted(jnp.cumsum(lengths), jnp.arange(rows * top), side="right").astype(jnp.int32)
    table = labels.reshape(top, rows).T
    table = table[jax.random.permutation(jax.random.fold_in(own, 1), rows)]
    offset_by = jax.random.randint(jax.random.fold_in(own, 2), (rows, 1), 0, top)
    return jnp.take_along_axis(table, (jnp.arange(top)[None, :] + offset_by) % top, axis=1)


def load_shares(amount, total, limit, skew, full):
    weights = [(1 << 20) // math.isqrt(rank ** skew) + 1 for rank in range(1, amount + 1)]
    largest = limit if full else min(limit, max(-(-total // amount), total * weights[0] // sum(weights)))
    least = 1 if total - largest >= amount - 1 else 0
    counts, rest = [largest] + [least] * (amount - 1), total - largest - least * (amount - 1)
    while rest > 0:
        candidates = [i for i in range(1, amount) if counts[i] < largest] or [i for i in range(1, amount) if counts[i] < limit]
        whole, remaining = sum([weights[i] for i in candidates]), rest
        for i in candidates:
            addition = min(limit - counts[i], max(1, remaining * weights[i] // whole), rest)
            counts[i] = counts[i] + addition
            rest = rest - addition
    return np.array(counts)


def centred(stream_key, dims, width, reach, split=(), kind=jnp.bfloat16):
    entries = jax.random.normal(stream_key, dims, jnp.float32) * width
    if len(split) > 0:
        entries = steps_of(stream_key, dims, split, -0.22, 0.18) * entries
    return jnp.clip(entries, min=-reach, max=reach).astype(kind)


def setup_inputs(seed: int = 0) -> dict:
    arg_keys = jax.random.split(jax.random.key(seed), 10)
    spectrum = jnp.clip(jnp.exp(math.log(4.0) - 2.7725887 * jax.random.uniform(arg_keys[0], (K, P_SIZE), jnp.float32) ** steps_of(arg_keys[0], (K, P_SIZE), ((1, 128),), -0.2, 0.2)), 0.25, 4.0)
    source_weights = centred(arg_keys[1], (4, K, K), K ** -0.5, 0.1875)
    drift_weights = centred(arg_keys[2], (2 * LEV, K), K ** -0.5, 0.1875)
    courant = jnp.clip(jax.random.uniform(arg_keys[3], (2, K), jnp.float32, -0.45, 0.45), -0.45, 0.45)
    point_tile_keys = jax.random.split(jax.random.fold_in(arg_keys[4], 1), P_SIZE // PT_DEV)
    point_tile_turns = jax.random.permutation(jax.random.fold_in(arg_keys[4], 3), P_SIZE // PT_DEV)
    point_tile = jax.vmap(lambda own, number: shared_out(jax.random.fold_in(arg_keys[4], 2), own, number, PT_DEV, DEVICES, 1, CAP, 2))(point_tile_keys, point_tile_turns).reshape((P_SIZE, 1))
    point_cell = touch_ends(jax.random.randint(arg_keys[5], (P_SIZE,), 0, OX * OY), jax.random.fold_in(arg_keys[5], 1), 0, (OX * OY) - 1).astype(jnp.int32)
    wave_land = touch_ends((jax.random.randint(arg_keys[6], (P_SIZE,), 0, 8) < 7).astype(jnp.int32), jax.random.fold_in(arg_keys[6], 1), 0, 1)
    ocean_vel = centred(arg_keys[7], (2, LEV, NOX, NOY), 1.0, 6.0, ((2, 16), (3, 8)), jnp.float32)
    ocean_land = touch_ends((jax.random.randint(arg_keys[8], (NOX, NOY), 0, 10) < 9).astype(jnp.int32), jax.random.fold_in(arg_keys[8], 1), 0, 1)
    return dict(spectrum=spectrum, source_weights=source_weights, drift_weights=drift_weights, courant=courant, point_tile=point_tile, point_cell=point_cell, wave_land=wave_land, ocean_vel=ocean_vel, ocean_land=ocean_land)


SOURCE_RATE = 0.1
REFRACT_RATE = 0.1
VISCOUS = 0.2
CORIOLIS = 0.1


def upwind(density, speed_x, speed_y):
    zeros_row = jnp.zeros_like(density[:, :1, :])
    east_cell = jnp.concatenate([density[:, 1:, :], zeros_row], axis=1)
    flux_x = jnp.maximum(speed_x, 0.0) * density + jnp.minimum(speed_x, 0.0) * east_cell
    inflow_x = jnp.concatenate([zeros_row, flux_x[:, :-1, :]], axis=1)
    zeros_col = jnp.zeros_like(density[:, :, :1])
    north_cell = jnp.concatenate([density[:, :, 1:], zeros_col], axis=2)
    flux_y = jnp.maximum(speed_y, 0.0) * density + jnp.minimum(speed_y, 0.0) * north_cell
    inflow_y = jnp.concatenate([zeros_col, flux_y[:, :, :-1]], axis=2)
    return density - (flux_x - inflow_x) - (flux_y - inflow_y)


def ocean_substep(padded_u, padded_v, force_u, force_v, sea_mask):
    inner_u = padded_u[:, 1:-1, 1:-1]
    inner_v = padded_v[:, 1:-1, 1:-1]
    lap_u = padded_u[:, 2:, 1:-1] + padded_u[:, :-2, 1:-1] + padded_u[:, 1:-1, 2:] + padded_u[:, 1:-1, :-2] - 4.0 * inner_u
    lap_v = padded_v[:, 2:, 1:-1] + padded_v[:, :-2, 1:-1] + padded_v[:, 1:-1, 2:] + padded_v[:, 1:-1, :-2] - 4.0 * inner_v
    new_u = sea_mask * (inner_u + VISCOUS * lap_u + CORIOLIS * (inner_v + force_v))
    new_v = sea_mask * (inner_v + VISCOUS * lap_v - CORIOLIS * (inner_u + force_u))
    return new_u, new_v


def reference(spectrum, source_weights, drift_weights, courant, point_tile, point_cell, wave_land, ocean_vel, ocean_land):
    groups = DEVICES
    block_bins = K // groups
    row_count = N_MP * N_GX
    tile_ids = point_tile[:, 0]
    cell_rows = (tile_ids // N_GY) * OX + point_cell // OY
    cell_cols = (tile_ids % N_GY) * OY + point_cell % OY
    sea_wave = wave_land.astype(jnp.float32)
    sea_mask = ocean_land.astype(jnp.float32)[None]
    east_u = ocean_vel[0]
    north_v = ocean_vel[1]
    energy = spectrum
    speeds = courant.reshape(2, groups, block_bins)
    block_ids = jnp.arange(groups, dtype=jnp.int32)
    drift_wide = drift_weights.astype(jnp.float32)
    for number in range(NSTEP):
        coarse = energy.astype(jnp.bfloat16).astype(jnp.float32)
        drift_rows = jnp.dot(drift_wide, coarse, precision=lax.Precision.HIGHEST, preferred_element_type=jnp.float32)
        forcing = jnp.zeros((2 * LEV, row_count * OX, N_GY * OY), jnp.float32).at[:, cell_rows, cell_cols].add(drift_rows)
        current_u = east_u[0, cell_rows, cell_cols]
        current_v = north_v[0, cell_rows, cell_cols]
        for repeat in range(2):
            padded_u = jnp.pad(east_u, ((0, 0), (1, 1), (1, 1)))
            padded_v = jnp.pad(north_v, ((0, 0), (1, 1), (1, 1)))
            east_u, north_v = ocean_substep(padded_u, padded_v, forcing[:LEV], forcing[LEV:], sea_mask)

        def source_block(block_index):
            block_weights = lax.dynamic_slice_in_dim(source_weights, block_index * block_bins, block_bins, 1)
            block_weights = block_weights.reshape(4 * block_bins, K).astype(jnp.float32)
            linear = jnp.dot(block_weights, coarse, precision=lax.Precision.HIGHEST, preferred_element_type=jnp.float32)
            linear = linear.reshape(4, block_bins, -1)
            previous = lax.dynamic_slice_in_dim(energy, block_index * block_bins, block_bins, 0)
            return sea_wave * (previous + SOURCE_RATE * linear[0] * linear[1] + REFRACT_RATE * (current_u * linear[2] + current_v * linear[3]))

        source_step = lax.map(source_block, block_ids).reshape(K, -1)
        wave_grid = source_step.reshape(K, row_count, N_GY, PBX, PBY).transpose(0, 1, 3, 2, 4)
        wave_grid = wave_grid.reshape(groups, block_bins, row_count * PBX, N_GY * PBY)

        def move_block(block_index):
            return upwind(wave_grid[block_index], speeds[0, block_index][:, None, None], speeds[1, block_index][:, None, None])

        advected = lax.map(move_block, block_ids)
        advected = advected.reshape(K, row_count, PBX, N_GY, PBY).transpose(0, 1, 3, 2, 4).reshape(K, -1)
        energy = advected * sea_wave
    return energy, jnp.stack([east_u, north_v])
```

```python
import jax
import jax.numpy as jnp
from jax import lax
from jax.experimental import pallas as pl
from jax.experimental.pallas import tpu as pltpu
from jax.sharding import PartitionSpec as P

ALL = ("mp", "gx", "gy")
F32 = jnp.float32
BF16 = jnp.bfloat16
MESH = pl.DeviceIdType.MESH

BINS = 1152
PTS = 128
LEV = 32
PLANES = 64
DEVS = 128
ROWS = 16
COLS = 8
PAD = 144
CHUNK = 72
MROWS = 384


def near(a):
    return min(a, 4 - a)


OFFSETS = sorted(
    [
        (dx, dy, dz, dc)
        for dx in range(4)
        for dy in range(4)
        for dz in range(4)
        for dc in range(2)
        if (dx, dy, dz, dc) != (0, 0, 0, 0)
    ],
    key=lambda d: (-(near(d[0]) + near(d[1]) + near(d[2])), d),
)


def split(x):
    high = x.astype(BF16)
    low = (x - high.astype(F32)).astype(BF16)
    return high, low


def dot_nt(a, b):
    return lax.dot_general(a, b, (((1,), (1,)), ((), ())), preferred_element_type=F32)


def dot_tn(a, b):
    return lax.dot_general(a, b, (((0,), (0,)), ((), ())), preferred_element_type=F32)


def dot_nn(a, b):
    return jnp.dot(a, b, preferred_element_type=F32)


def kernel(
    spec_h, w_h, dw_h, cour_v, tile_v, cell_v, land_v, vel_h, oland_h,
    eout_h, oout_h,
    e_v, c_v, g_v, lin_v, w_v, dw_v, cx_v, cy_v, oa_v, ob_v, f_v, sea_v, ol_v,
    q_v, rt_v, rs_v, cc_v, at_v,
    s1, r1, s2, r2, s3, r3, s4, r4,
    rowp, rowr, colp, colr, hc_v,
    wrp, wrr, wcp, wcr,
    in_sem, w_sem, out_sem, a_send, a_recv, h_send, h_recv, g_send, g_recv,
):
    mp, gx, gy = lax.axis_index("mp"), lax.axis_index("gx"), lax.axis_index("gy")
    row = mp * 8 + gx
    me = row * 8 + gy
    px, pz, py, pc = mp * 2 + gx % 2, gx // 2, gy // 2, gy % 2

    in_e = pltpu.make_async_copy(spec_h, e_v, in_sem.at[0])
    in_dw = pltpu.make_async_copy(dw_h, dw_v, in_sem.at[1])
    in_ol = pltpu.make_async_copy(oland_h, ol_v, in_sem.at[2])
    in_u = pltpu.make_async_copy(vel_h, oa_v.at[:, pl.ds(8, 128), :], in_sem.at[3])
    in_e.start()
    in_dw.start()
    in_u.start()
    in_ol.start()
    in_w = [pltpu.make_async_copy(w_h.at[m], w_v.at[m], w_sem.at[m]) for m in range(4)]
    for copy in in_w:
        copy.start()

    barrier = pltpu.get_barrier_semaphore()

    def greet(i, carry):
        p = (me + i) % DEVS
        pl.semaphore_signal(
            barrier, inc=1, device_id=(p // 64, (p // 8) % 8, p % 8), device_id_type=MESH
        )
        return carry

    lax.fori_loop(1, DEVS, greet, 0)

    lane = lax.broadcasted_iota(jnp.int32, (128, 128), 1)
    sub = lax.broadcasted_iota(jnp.int32, (128, 128), 0)

    def exchange_all(n, src, dst):
        for dx, dy, dz, dc in OFFSETS:
            tx, ty, tz, tc = (px + dx) % 4, (py + dy) % 4, (pz + dz) % 4, (pc + dc) % 2
            to = (tx // 2, tz * 2 + tx % 2, ty * 2 + tc)
            peer = (to[0] * 8 + to[1]) * 8 + to[2]
            pltpu.make_async_remote_copy(
                src_ref=src.at[peer], dst_ref=dst.at[me],
                send_sem=a_send.at[n], recv_sem=a_recv.at[n],
                device_id=to, device_id_type=MESH,
            ).start()
        dst[pl.ds(me, 1)] = src[pl.ds(me, 1)]

    def exchange_sent(n, src):
        block = src.at[pl.ds(0, DEVS - 1)]
        pltpu.make_async_copy(block, block, a_send.at[n]).wait()

    def exchange_come(n, dst):
        block = dst.at[pl.ds(0, DEVS - 1)]
        pltpu.make_async_copy(block, block, a_recv.at[n]).wait()

    up, down = (row + ROWS - 1) % ROWS, (row + 1) % ROWS
    left, right = (gy + COLS - 1) % COLS, (gy + 1) % COLS
    at_up, at_down = (up // 8, up % 8, gy), (down // 8, down % 8, gy)
    at_left, at_right = (mp, gx, left), (mp, gx, right)

    def halo_copies(rows_out, rows_in, cols_out, cols_in, ss, rs, n):
        def one(k, src, dst, to):
            return pltpu.make_async_remote_copy(
                src_ref=src, dst_ref=dst, send_sem=ss.at[n, k], recv_sem=rs.at[n, k],
                device_id=to, device_id_type=MESH,
            )

        return [
            one(0, rows_out.at[0], rows_in.at[1], at_up),
            one(1, rows_out.at[1], rows_in.at[0], at_down),
            one(2, cols_out, cols_in.at[1], at_left),
            one(3, cols_out, cols_in.at[0], at_right),
        ]

    ocean_halo = [
        halo_copies(rowp.at[n], rowr.at[n], colp.at[n], colr.at[n], h_send, h_recv, n)
        for n in range(4)
    ]
    wave_halo = [
        halo_copies(wrp.at[n], wrr.at[n], wcp.at[n], wcr.at[n], g_send, g_recv, n)
        for n in range(2)
    ]
    has_up = (row > 0).astype(F32)
    has_down = (row < ROWS - 1).astype(F32)
    has_left = (gy > 0).astype(F32)
    has_right = (gy < COLS - 1).astype(F32)

    tile_row = jnp.broadcast_to(tile_v[...], (128, 128))
    tile_col = tile_row.T
    before = jnp.where((tile_row == tile_col) & (sub < lane), 1.0, 0.0)
    rank = jnp.sum(before, axis=0, keepdims=True)
    for r in range(2):
        mine = (tile_row == sub) & (jnp.broadcast_to(rank, (128, 128)) == float(r))
        q_v[r] = jnp.where(mine, 1.0, 0.0).astype(BF16)

    def drift_out(dst):
        d = dot_nn(dw_v[...], c_v[...])
        extra = jnp.broadcast_to((cell_v[...] + 1).astype(F32), (64, 128))
        high, low = split(jnp.concatenate([d, extra], axis=0))
        for r in range(2):
            dst[:, r, :] = dot_nt(q_v[r], high) + dot_nt(q_v[r], low)

    in_e.wait()
    in_dw.wait()
    c_v[...] = e_v[...].astype(BF16)
    drift_out(s1)

    for b in range(BINS // 128):
        block = pl.ds(b * 128, 128)
        cx_v[block, :] = jnp.broadcast_to(cour_v[0:1, block], (128, 128)).T
        cy_v[block, :] = jnp.broadcast_to(cour_v[1:2, block], (128, 128)).T

    in_ol.wait()
    sea_v[...] = ol_v[...].astype(F32) * 0.2
    in_u.wait()

    def insert(cols, x, p):
        here = (lane // 2) == p
        return jnp.where(here, pltpu.roll(x, 2 * p + 1, 1), cols)

    def pack_plane(n, p, x, cols):
        rowp[n, 0, pl.ds(p, 1), :] = x[0:1]
        rowp[n, 1, pl.ds(p, 1), :] = x[127:128]
        return insert(cols, x, p)

    def pack_first(p, cols):
        return pack_plane(0, p, oa_v[p, 8:136, :], cols)

    colp[0] = lax.fori_loop(0, PLANES, pack_first, jnp.zeros((128, 128), F32))

    def linear(first, last):
        def one(i, carry):
            m, b = i // 3, i % 3
            rows = pl.ds(pl.multiple_of(b * MROWS, MROWS), MROWS)
            lin_v[m, rows, :] = dot_nn(w_v[m, rows, :], c_v[...])
            return carry

        lax.fori_loop(first, last, one, 0)

    in_w[0].wait()
    linear(0, 3)
    pl.semaphore_wait(barrier, DEVS - 1)

    exchange_all(0, s1, r1)
    for copy in ocean_halo[0]:
        copy.start()
    for copy in in_w[1:]:
        copy.wait()
    linear(3, 12)

    exchange_come(0, r1)

    def arrived(src):
        return jnp.concatenate([src[:, 0, :], src[:, 1, :]], axis=0)

    a = arrived(r1)
    at = a.T
    at_v[...] = at[0:PLANES] * 0.5
    cell_t = at[64:65, :].astype(jnp.int32) - 1
    wide = lax.broadcasted_iota(jnp.int32, (128, 256), 0)
    rt_v[...] = jnp.where(wide == jnp.broadcast_to(cell_t >> 7, (128, 256)), 1.0, 0.0).astype(BF16)
    cell_c = jnp.broadcast_to(a[:, 64:65], (256, 128)).astype(jnp.int32) - 1
    tall = lax.broadcasted_iota(jnp.int32, (256, 128), 1)
    rs_v[...] = jnp.where(tall == (cell_c >> 7), 1.0, 0.0).astype(BF16)
    cc_v[...] = jnp.where(tall == (cell_c & 127), 1.0, 0.0).astype(BF16)

    def currents_out(ocean, dst):
        found = []
        for f in range(2):
            high, low = split(ocean[f * LEV, 8:136, :])
            x = dot_nn(rs_v[...], high) + dot_nn(rs_v[...], low)
            found.append(jnp.sum(x * cc_v[...].astype(F32), axis=1, keepdims=True))
        both = jnp.where(tall == 0, found[0], jnp.where(tall == 1, found[1], 0.0))
        dst[:, 0, :] = both[0:128]
        dst[:, 1, :] = both[128:256]

    currents_out(oa_v, s2)
    exchange_all(1, s2, r2)

    def forcing():
        def one(p, carry):
            high, low = split(jnp.broadcast_to(at_v[pl.ds(p, 1), :], (16, 256)))
            high = jnp.broadcast_to(high[0:1], (128, 256))
            low = jnp.broadcast_to(low[0:1], (128, 256))
            f_v[p] = dot_nn(rt_v[...] * high, cc_v[...]) + dot_nn(rt_v[...] * low, cc_v[...])
            return carry

        lax.fori_loop(0, PLANES, one, 0)

    def substep(n, src, dst, pack):
        for copy in ocean_halo[n]:
            copy.wait()
        even = (lane % 2) == 0
        hc_v[...] = jnp.where(
            even, colr[n, 0] * has_left, pltpu.roll(colr[n, 1], 126, 1) * has_right
        )

        def around(p):
            src[p, 7:8, :] = rowr[n, 0, pl.ds(p, 1), :] * has_up
            src[p, 136:137, :] = rowr[n, 1, pl.ds(p, 1), :] * has_down
            x = src[p, 8:136, :]
            edge = pltpu.roll(hc_v[...], (128 - 2 * p) % 128, 1)
            west = jnp.where(lane == 0, edge, pltpu.roll(x, 1, 1))
            east = jnp.where(lane == 127, edge, pltpu.roll(x, 127, 1))
            return x, (src[p, 7:135, :] + src[p, 9:137, :]) + (west + east) + x

        def one(l, cols):
            u, su = around(l)
            v, sv = around(LEV + l)
            un = sea_v[...] * (su + 0.5 * v + f_v[LEV + l])
            vn = sea_v[...] * (sv - 0.5 * u - f_v[l])
            dst[l, 8:136, :] = un
            dst[LEV + l, 8:136, :] = vn
            if pack:
                cols = pack_plane(n + 1, l, un, cols)
                cols = pack_plane(n + 1, LEV + l, vn, cols)
            return cols

        cols = lax.fori_loop(0, LEV, one, jnp.zeros((128, 128), F32))
        if pack:
            colp[n + 1] = cols
            for copy in ocean_halo[n + 1]:
                copy.start()

    sea_row = land_v[...].astype(F32)
    lane_c = lax.broadcasted_iota(jnp.int32, (CHUNK, 128), 1)
    seg = lane_c // 32
    pos = lane_c % 32

    def grow(n, src):
        exchange_come(2 * n + 1 if n == 0 else 3, src)
        now = jnp.zeros((128, 128), F32)
        for r in range(2):
            high, low = split(src[:, r, :])
            now = now + dot_tn(high, q_v[r]) + dot_tn(low, q_v[r])
        cu, cv = now[0:1], now[1:2]

        def one(k, carry):
            first = jnp.zeros((CHUNK, 128), F32)
            last = jnp.zeros((CHUNK, 128), F32)
            cols = carry
            for q in range(4):
                rows = pl.ds(pl.multiple_of(288 * q + CHUNK * k, 8), CHUNK)
                g = sea_row * (
                    e_v[rows, :]
                    + 0.1 * lin_v[0, rows, :] * lin_v[1, rows, :]
                    + 0.1 * (cu * lin_v[2, rows, :] + cv * lin_v[3, rows, :])
                )
                g_v[rows, :] = g
                first = jnp.where(seg == q, pltpu.roll(g, 32 * q, 1) if q else g, first)
                last = jnp.where(seg == q, pltpu.roll(g, (32 * q + 32) % 128, 1) if q < 3 else g, last)
                group = 4 * q + k
                cols = jnp.where(pos // 2 == group, pltpu.roll(g, 2 * group + 1, 1), cols)
            part = pl.ds(pl.multiple_of(CHUNK * k, 8), CHUNK)
            wrp[n, 0, part, :] = first
            wrp[n, 1, part, :] = last
            return cols

        wcp[n] = lax.fori_loop(0, 4, one, jnp.zeros((CHUNK, 128), F32))
        for copy in wave_halo[n]:
            copy.start()

    def advect(n):
        for copy in wave_halo[n]:
            copy.wait()
        cols = jnp.where(
            lane_c % 2 == 0,
            pltpu.roll(wcr[n, 0], 96, 1) * has_left,
            pltpu.roll(wcr[n, 1], 30, 1) * has_right,
        )
        flow_x = jnp.where(seg == 0, has_up, 1.0)
        flow_y = jnp.where(pos == 0, has_left, 1.0)

        def one(k, carry):
            part = pl.ds(pl.multiple_of(CHUNK * k, 8), CHUNK)
            above = wrr[n, 0, part, :] * has_up
            below = wrr[n, 1, part, :] * has_down
            for q in range(4):
                rows = pl.ds(pl.multiple_of(288 * q + CHUNK * k, 8), CHUNK)
                group = 4 * q + k
                g = g_v[rows, :]
                cx, cy = cx_v[rows, :], cy_v[rows, :]
                edge = pltpu.roll(cols, (128 - 2 * group) % 128, 1)
                g_down = jnp.where(
                    seg == 3, pltpu.roll(below, (96 - 32 * q) % 128, 1), pltpu.roll(g, 96, 1)
                )
                g_up = jnp.where(
                    seg == 0, pltpu.roll(above, (128 - 32 * q) % 128, 1), pltpu.roll(g, 32, 1)
                )
                g_right = jnp.where(pos == 31, edge, pltpu.roll(g, 127, 1))
                g_left = jnp.where(pos == 0, edge, pltpu.roll(g, 1, 1))
                px_, nx_ = jnp.maximum(cx, 0.0), jnp.minimum(cx, 0.0)
                py_, ny_ = jnp.maximum(cy, 0.0), jnp.minimum(cy, 0.0)
                out_x = px_ * g + nx_ * g_down
                in_x = flow_x * (px_ * g_up + nx_ * g)
                out_y = py_ * g + ny_ * g_right
                in_y = flow_y * (py_ * g_left + ny_ * g)
                e_v[rows, :] = sea_row * (g - (out_x - in_x) - (out_y - in_y))
            return carry

        lax.fori_loop(0, 4, one, 0)

    forcing()
    substep(0, oa_v, ob_v, True)
    grow(0, r2)
    substep(1, ob_v, oa_v, True)
    currents_out(oa_v, s4)
    exchange_all(3, s4, r4)
    advect(0)
    c_v[...] = e_v[...].astype(BF16)
    drift_out(s3)
    exchange_all(2, s3, r3)
    linear(0, 12)
    grow(1, r4)
    exchange_come(2, r3)
    at_v[...] = arrived(r3).T[0:PLANES] * 0.5
    forcing()
    substep(2, oa_v, ob_v, True)
    advect(1)
    out_e = pltpu.make_async_copy(e_v, eout_h, out_sem.at[0])
    out_e.start()
    substep(3, ob_v, oa_v, False)
    out_u = pltpu.make_async_copy(oa_v.at[:, pl.ds(8, 128), :], oout_h, out_sem.at[1])
    out_u.start()
    for n, src in enumerate((s1, s2, s3, s4)):
        exchange_sent(n, src)
    out_e.wait()
    out_u.wait()


def step(spectrum, weights, drift, courant, tile, cell, land, vel, oland):
    small = pl.BlockSpec(memory_space=pltpu.VMEM)
    far = pl.BlockSpec(memory_space=pl.ANY)
    v = pltpu.VMEM
    d = pltpu.SemaphoreType.DMA
    block = v((DEVS, 2, 128), F32)
    e, o = pl.pallas_call(
        kernel,
        out_shape=(
            jax.ShapeDtypeStruct((BINS, PTS), F32),
            jax.ShapeDtypeStruct((PLANES, 128, 128), F32),
        ),
        in_specs=[far, far, far, small, small, small, small, far, far],
        out_specs=(far, far),
        scratch_shapes=[
            v((BINS, 128), F32), v((BINS, 128), BF16), v((BINS, 128), F32),
            v((4, BINS, 128), F32), v((4, BINS, BINS), BF16), v((PLANES, BINS), BF16),
            v((BINS, 128), F32), v((BINS, 128), F32),
            v((PLANES, PAD, 128), F32), v((PLANES, PAD, 128), F32),
            v((PLANES, 128, 128), F32), v((128, 128), F32), v((128, 128), jnp.int32),
            v((2, 128, 128), BF16), v((128, 256), BF16), v((256, 128), BF16),
            v((256, 128), BF16), v((PLANES, 256), F32),
            block, block, block, block, block, block, block, block,
            v((4, 2, PLANES, 128), F32), v((4, 2, PLANES, 128), F32),
            v((4, 128, 128), F32), v((4, 2, 128, 128), F32), v((128, 128), F32),
            v((2, 2, 288, 128), F32), v((2, 2, 288, 128), F32),
            v((2, CHUNK, 128), F32), v((2, 2, CHUNK, 128), F32),
            d((4,)), d((4,)), d((2,)), d((4,)), d((4,)),
            d((4, 4)), d((4, 4)), d((2, 4)), d((2, 4)),
        ],
        name="coupled",
        compiler_params=pltpu.CompilerParams(
            collective_id=0, has_side_effects=True, vmem_limit_bytes=60 * 1024 * 1024
        ),
    )(
        spectrum, weights, drift, courant,
        tile.reshape(1, PTS), cell.reshape(1, PTS), land.reshape(1, PTS),
        vel.reshape(PLANES, 128, 128), oland,
    )
    return e, o.reshape(2, LEV, 128, 128)


def solution(mesh):
    ocean = P(None, None, ("mp", "gx"), "gy")
    return jax.shard_map(
        step,
        mesh=mesh,
        in_specs=(
            P(None, ALL), P(), P(), P(), P(ALL, None), P(ALL), P(ALL),
            ocean, P(("mp", "gx"), "gy"),
        ),
        out_specs=(P(None, ALL), ocean),
        check_vma=False,
    )
```

```python
import jax
import jax.numpy as jnp
from jax import lax
from jax.experimental import pallas as pl
from jax.experimental.pallas import tpu as pltpu
from jax.sharding import PartitionSpec as P

ALL = ("mp", "gx", "gy")
F32 = jnp.float32
BF16 = jnp.bfloat16
MESH = pl.DeviceIdType.MESH

BINS = 1152
PTS = 128
LEV = 32
PLANES = 64
DEVS = 128
ROWS = 16
COLS = 8
PAD = 144
CHUNK = 72
MROWS = 384
STRIP = 128
UNROLL = 4


def near(a):
    return min(a, 4 - a)


OFFSETS = sorted(
    [
        (dx, dy, dz, dc)
        for dx in range(4)
        for dy in range(4)
        for dz in range(4)
        for dc in range(2)
        if (dx, dy, dz, dc) != (0, 0, 0, 0)
    ],
    key=lambda d: (-(near(d[0]) + near(d[1]) + near(d[2])), d),
)


def place(x, y, z, core):
    return (x // 2, z * 2 + x % 2, y * 2 + core)


def split(x):
    high = x.astype(BF16)
    low = (x - high.astype(F32)).astype(BF16)
    return high, low


def dot_nt(a, b):
    return lax.dot_general(a, b, (((1,), (1,)), ((), ())), preferred_element_type=F32)


def dot_tn(a, b):
    return lax.dot_general(a, b, (((0,), (0,)), ((), ())), preferred_element_type=F32)


def dot_nn(a, b):
    return jnp.dot(a, b, preferred_element_type=F32)


def kernel(
    spec_h, w_h, dw_h, cour_v, tile_v, cell_v, land_v, vel_h, oland_h,
    eout_h, oout_h,
    e_v, c_v, g_v, lin_v, w_v, dw_v, cx_v, cy_v, oa_v, ob_v, f_v, sea_v, ol_v, tri_v,
    q_v, rt_v, rs_v, cc_v, at_v,
    s1, r1, s2, r2, s3, r3, s4, r4,
    rowp, rowr, colp, colr, hc_v,
    wrp, wrr, wcp, wcr,
    in_sem, w_sem, out_sem, a_send, a_recv, h_send, h_recv, g_send, g_recv,
):
    mp, gx, gy = lax.axis_index("mp"), lax.axis_index("gx"), lax.axis_index("gy")
    row = mp * 8 + gx
    me = row * 8 + gy
    px, pz, py, pc = mp * 2 + gx % 2, gx // 2, gy // 2, gy % 2

    in_e = pltpu.make_async_copy(spec_h, e_v, in_sem.at[0])
    in_dw = pltpu.make_async_copy(dw_h, dw_v, in_sem.at[1])
    in_ol = pltpu.make_async_copy(oland_h, ol_v, in_sem.at[2])
    in_u = pltpu.make_async_copy(vel_h, oa_v.at[:, pl.ds(8, 128), :], in_sem.at[3])
    in_e.start()
    in_dw.start()
    in_u.start()
    in_ol.start()
    in_w = [pltpu.make_async_copy(w_h.at[m], w_v.at[m], w_sem.at[m]) for m in range(4)]
    for copy in in_w:
        copy.start()

    barrier = pltpu.get_barrier_semaphore()

    for dx, dy, dz, dc in OFFSETS:
        to = place((px + dx) % 4, (py + dy) % 4, (pz + dz) % 4, (pc + dc) % 2)
        pl.semaphore_signal(barrier, inc=1, device_id=to, device_id_type=MESH)

    lane = lax.broadcasted_iota(jnp.int32, (128, 128), 1)
    sub = lax.broadcasted_iota(jnp.int32, (128, 128), 0)

    def exchange_all(n, src, dst):
        for dx, dy, dz, dc in OFFSETS:
            to = place((px + dx) % 4, (py + dy) % 4, (pz + dz) % 4, (pc + dc) % 2)
            peer = (to[0] * 8 + to[1]) * 8 + to[2]
            pltpu.make_async_remote_copy(
                src_ref=src.at[peer], dst_ref=dst.at[me],
                send_sem=a_send.at[n], recv_sem=a_recv.at[n],
                device_id=to, device_id_type=MESH,
            ).start()
        dst[pl.ds(me, 1)] = src[pl.ds(me, 1)]

    def exchange_sent(n, src):
        block = src.at[pl.ds(0, DEVS - 1)]
        pltpu.make_async_copy(block, block, a_send.at[n]).wait()

    def exchange_come(n, dst):
        block = dst.at[pl.ds(0, DEVS - 1)]
        pltpu.make_async_copy(block, block, a_recv.at[n]).wait()

    up, down = (row + ROWS - 1) % ROWS, (row + 1) % ROWS
    left, right = (gy + COLS - 1) % COLS, (gy + 1) % COLS
    at_up, at_down = (up // 8, up % 8, gy), (down // 8, down % 8, gy)
    at_left, at_right = (mp, gx, left), (mp, gx, right)

    def halo_copies(rows_out, rows_in, cols_out, cols_in, ss, rs, n):
        def one(k, src, dst, to):
            return pltpu.make_async_remote_copy(
                src_ref=src, dst_ref=dst, send_sem=ss.at[n, k], recv_sem=rs.at[n, k],
                device_id=to, device_id_type=MESH,
            )

        return [
            one(0, rows_out.at[0], rows_in.at[1], at_up),
            one(1, rows_out.at[1], rows_in.at[0], at_down),
            one(2, cols_out, cols_in.at[1], at_left),
            one(3, cols_out, cols_in.at[0], at_right),
        ]

    ocean_halo = [
        halo_copies(rowp.at[n], rowr.at[n], colp.at[n], colr.at[n], h_send, h_recv, n)
        for n in range(4)
    ]
    wave_halo = [
        halo_copies(wrp.at[n], wrr.at[n], wcp.at[n], wcr.at[n], g_send, g_recv, n)
        for n in range(2)
    ]
    has_up = (row > 0).astype(F32)
    has_down = (row < ROWS - 1).astype(F32)
    has_left = (gy > 0).astype(F32)
    has_right = (gy < COLS - 1).astype(F32)

    tile_row = jnp.broadcast_to(tile_v[...], (128, 128))
    tile_col = tile_row.T
    before = jnp.where((tile_row == tile_col) & (sub < lane), 1.0, 0.0)
    rank = jnp.sum(before, axis=0, keepdims=True)
    for r in range(2):
        mine = (tile_row == sub) & (jnp.broadcast_to(rank, (128, 128)) == float(r))
        q_v[r] = jnp.where(mine, 1.0, 0.0).astype(BF16)

    def drift_out(dst):
        d = dot_nn(dw_v[...], c_v[...])
        extra = jnp.broadcast_to((cell_v[...] + 1).astype(F32), (64, 128))
        high, low = split(jnp.concatenate([d, extra], axis=0))
        for r in range(2):
            dst[:, r, :] = dot_nt(q_v[r], high) + dot_nt(q_v[r], low)

    in_e.wait()
    in_dw.wait()
    c_v[...] = e_v[...].astype(BF16)
    drift_out(s1)

    for b in range(BINS // 128):
        block = pl.ds(b * 128, 128)
        cx_v[block, :] = jnp.broadcast_to(cour_v[0:1, block], (128, 128)).T
        cy_v[block, :] = jnp.broadcast_to(cour_v[1:2, block], (128, 128)).T

    deep = lax.broadcasted_iota(jnp.int32, (256, 128), 0) & 127
    tall = lax.broadcasted_iota(jnp.int32, (256, 128), 1)
    tri_v[...] = jnp.where((deep - tall == 1) | (tall - deep == 1), 1.0, 0.0).astype(BF16)
    in_ol.wait()
    sea_v[...] = ol_v[...].astype(F32) * 0.2

    lane_s = lax.broadcasted_iota(jnp.int32, (STRIP, 128), 1)

    def pack_plane(n, p, s, x):
        if s == 0:
            rowp[n, 0, pl.ds(p, 1), :] = x[0:1]
        if s == 128 // STRIP - 1:
            rowp[n, 1, pl.ds(p, 1), :] = x[STRIP - 1 : STRIP]
        pltpu.store(
            colp.at[n, pl.ds(s * STRIP, STRIP), :],
            pltpu.roll(x, 2 * p + 1, 1),
            mask=(lane_s >> 1) == p,
        )

    def pack_first(p, carry):
        for s in range(128 // STRIP):
            pack_plane(0, p, s, oa_v[p, 8 + s * STRIP : 8 + (s + 1) * STRIP, :])
        return carry

    def pack_start():
        lax.fori_loop(0, PLANES, pack_first, 0, unroll=4)

    def linear(first, last):
        def one(i, carry):
            m, b = i // 3, i % 3
            rows = pl.ds(pl.multiple_of(b * MROWS, MROWS), MROWS)
            lin_v[m, rows, :] = dot_nn(w_v[m, rows, :], c_v[...])
            return carry

        lax.fori_loop(first, last, one, 0)

    in_w[0].wait()
    linear(0, 3)
    pl.semaphore_wait(barrier, DEVS - 1)
    exchange_all(0, s1, r1)
    in_u.wait()
    pack_start()
    for copy in ocean_halo[0]:
        copy.start()
    for copy in in_w[1:]:
        copy.wait()
    linear(3, 12)

    exchange_come(0, r1)

    def arrived(src):
        return jnp.concatenate([src[:, 0, :], src[:, 1, :]], axis=0)

    a = arrived(r1)
    at = a.T
    at_v[...] = at[0:PLANES] * 0.5
    cell_t = at[64:65, :].astype(jnp.int32) - 1
    wide = lax.broadcasted_iota(jnp.int32, (128, 256), 0)
    rt_v[...] = jnp.where(wide == jnp.broadcast_to(cell_t >> 7, (128, 256)), 1.0, 0.0).astype(BF16)
    cell_c = jnp.broadcast_to(a[:, 64:65], (256, 128)).astype(jnp.int32) - 1
    rs_v[...] = jnp.where(tall == (cell_c >> 7), 1.0, 0.0).astype(BF16)
    cc_v[...] = jnp.where(tall == (cell_c & 127), 1.0, 0.0).astype(BF16)

    def currents_out(ocean, dst):
        found = []
        for f in range(2):
            high, low = split(ocean[f * LEV, 8:136, :])
            x = dot_nn(rs_v[...], high) + dot_nn(rs_v[...], low)
            found.append(jnp.sum(x * cc_v[...].astype(F32), axis=1, keepdims=True))
        both = jnp.where(tall == 0, found[0], jnp.where(tall == 1, found[1], 0.0))
        dst[:, 0, :] = both[0:128]
        dst[:, 1, :] = both[128:256]

    currents_out(oa_v, s2)
    exchange_all(1, s2, r2)

    def forcing():
        def one(p, carry):
            high, low = split(jnp.broadcast_to(at_v[pl.ds(p, 1), :], (16, 256)))
            high = jnp.broadcast_to(high[0:1], (128, 256))
            low = jnp.broadcast_to(low[0:1], (128, 256))
            f_v[p] = dot_nn(rt_v[...] * high, cc_v[...]) + dot_nn(rt_v[...] * low, cc_v[...])
            return carry

        lax.fori_loop(0, PLANES, one, 0, unroll=16)

    def substep(n, src, dst, pack):
        for copy in ocean_halo[n]:
            copy.wait()
        src[:, 7, :] = rowr[n, 0] * has_up
        src[:, 136, :] = rowr[n, 1] * has_down
        even = (lane % 2) == 0
        hc_v[...] = jnp.where(
            even, colr[n, 0] * has_left, pltpu.roll(colr[n, 1], 126, 1) * has_right
        )

        brim = (lane == 0) | (lane == 127)

        def around(p):
            x = src[p, 8:136, :]
            high, low = split(x)
            across = dot_nn(jnp.concatenate([high, low], axis=1), tri_v[...])
            edge = jnp.where(brim, pltpu.roll(hc_v[...], (128 - 2 * p) % 128, 1), 0.0)
            return x, (src[p, 7:135, :] + src[p, 9:137, :]) + (x + edge) + across

        def one(l, carry):
            u, su = around(l)
            v, sv = around(LEV + l)
            un = sea_v[...] * (su + (0.5 * v + f_v[LEV + l]))
            vn = sea_v[...] * (sv - (0.5 * u + f_v[l]))
            dst[l, 8:136, :] = un
            dst[LEV + l, 8:136, :] = vn
            if pack:
                for s in range(128 // STRIP):
                    rows = slice(s * STRIP, (s + 1) * STRIP)
                    pack_plane(n + 1, l, s, un[rows])
                    pack_plane(n + 1, LEV + l, s, vn[rows])
            return carry

        lax.fori_loop(0, LEV, one, 0, unroll=UNROLL)
        if pack:
            for copy in ocean_halo[n + 1]:
                copy.start()

    sea_row = land_v[...].astype(F32)
    lane_c = lax.broadcasted_iota(jnp.int32, (CHUNK, 128), 1)
    seg = lane_c // 32
    pos = lane_c % 32

    def grow(n, src):
        exchange_come(2 * n + 1 if n == 0 else 3, src)
        now = jnp.zeros((128, 128), F32)
        for r in range(2):
            high, low = split(src[:, r, :])
            now = now + dot_tn(high, q_v[r]) + dot_tn(low, q_v[r])
        cu, cv = now[0:1], now[1:2]

        def one(k, carry):
            first = jnp.zeros((CHUNK, 128), F32)
            last = jnp.zeros((CHUNK, 128), F32)
            cols = carry
            for q in range(4):
                rows = pl.ds(pl.multiple_of(288 * q + CHUNK * k, 8), CHUNK)
                g = sea_row * (
                    e_v[rows, :]
                    + 0.1 * lin_v[0, rows, :] * lin_v[1, rows, :]
                    + 0.1 * (cu * lin_v[2, rows, :] + cv * lin_v[3, rows, :])
                )
                g_v[rows, :] = g
                first = jnp.where(seg == q, pltpu.roll(g, 32 * q, 1) if q else g, first)
                last = jnp.where(seg == q, pltpu.roll(g, (32 * q + 32) % 128, 1) if q < 3 else g, last)
                group = 4 * q + k
                cols = jnp.where(pos // 2 == group, pltpu.roll(g, 2 * group + 1, 1), cols)
            part = pl.ds(pl.multiple_of(CHUNK * k, 8), CHUNK)
            wrp[n, 0, part, :] = first
            wrp[n, 1, part, :] = last
            return cols

        wcp[n] = lax.fori_loop(0, 4, one, jnp.zeros((CHUNK, 128), F32))
        for copy in wave_halo[n]:
            copy.start()

    def advect(n):
        for copy in wave_halo[n]:
            copy.wait()
        cols = jnp.where(
            lane_c % 2 == 0,
            pltpu.roll(wcr[n, 0], 96, 1) * has_left,
            pltpu.roll(wcr[n, 1], 30, 1) * has_right,
        )
        flow_x = jnp.where(seg == 0, has_up, 1.0)
        flow_y = jnp.where(pos == 0, has_left, 1.0)

        def one(k, carry):
            part = pl.ds(pl.multiple_of(CHUNK * k, 8), CHUNK)
            above = wrr[n, 0, part, :] * has_up
            below = wrr[n, 1, part, :] * has_down
            for q in range(4):
                rows = pl.ds(pl.multiple_of(288 * q + CHUNK * k, 8), CHUNK)
                group = 4 * q + k
                g = g_v[rows, :]
                cx, cy = cx_v[rows, :], cy_v[rows, :]
                edge = pltpu.roll(cols, (128 - 2 * group) % 128, 1)
                g_down = jnp.where(
                    seg == 3, pltpu.roll(below, (96 - 32 * q) % 128, 1), pltpu.roll(g, 96, 1)
                )
                g_up = jnp.where(
                    seg == 0, pltpu.roll(above, (128 - 32 * q) % 128, 1), pltpu.roll(g, 32, 1)
                )
                g_right = jnp.where(pos == 31, edge, pltpu.roll(g, 127, 1))
                g_left = jnp.where(pos == 0, edge, pltpu.roll(g, 1, 1))
                px_, nx_ = jnp.maximum(cx, 0.0), jnp.minimum(cx, 0.0)
                py_, ny_ = jnp.maximum(cy, 0.0), jnp.minimum(cy, 0.0)
                out_x = px_ * g + nx_ * g_down
                in_x = flow_x * (px_ * g_up + nx_ * g)
                out_y = py_ * g + ny_ * g_right
                in_y = flow_y * (py_ * g_left + ny_ * g)
                e_v[rows, :] = sea_row * (g - (out_x - in_x) - (out_y - in_y))
            return carry

        lax.fori_loop(0, 4, one, 0)

    forcing()
    substep(0, oa_v, ob_v, True)
    grow(0, r2)
    substep(1, ob_v, oa_v, True)
    advect(0)
    c_v[...] = e_v[...].astype(BF16)
    drift_out(s3)
    exchange_all(2, s3, r3)
    currents_out(oa_v, s4)
    exchange_all(3, s4, r4)
    linear(0, 8)
    exchange_come(2, r3)
    at_v[...] = arrived(r3).T[0:PLANES] * 0.5
    forcing()
    substep(2, oa_v, ob_v, True)
    linear(8, 12)
    grow(1, r4)
    substep(3, ob_v, oa_v, False)
    out_u = pltpu.make_async_copy(oa_v.at[:, pl.ds(8, 128), :], oout_h, out_sem.at[1])
    out_u.start()
    advect(1)
    out_e = pltpu.make_async_copy(e_v, eout_h, out_sem.at[0])
    out_e.start()
    for n, src in enumerate((s1, s2, s3, s4)):
        exchange_sent(n, src)
    out_e.wait()
    out_u.wait()


def step(spectrum, weights, drift, courant, tile, cell, land, vel, oland):
    small = pl.BlockSpec(memory_space=pltpu.VMEM)
    far = pl.BlockSpec(memory_space=pl.ANY)
    v = pltpu.VMEM
    d = pltpu.SemaphoreType.DMA
    block = v((DEVS, 2, 128), F32)
    e, o = pl.pallas_call(
        kernel,
        out_shape=(
            jax.ShapeDtypeStruct((BINS, PTS), F32),
            jax.ShapeDtypeStruct((PLANES, 128, 128), F32),
        ),
        in_specs=[far, far, far, small, small, small, small, far, far],
        out_specs=(far, far),
        scratch_shapes=[
            v((BINS, 128), F32), v((BINS, 128), BF16), v((BINS, 128), F32),
            v((4, BINS, 128), F32), v((4, BINS, BINS), BF16), v((PLANES, BINS), BF16),
            v((BINS, 128), F32), v((BINS, 128), F32),
            v((PLANES, PAD, 128), F32), v((PLANES, PAD, 128), F32),
            v((PLANES, 128, 128), F32), v((128, 128), F32), v((128, 128), jnp.int32), v((256, 128), BF16),
            v((2, 128, 128), BF16), v((128, 256), BF16), v((256, 128), BF16),
            v((256, 128), BF16), v((PLANES, 256), F32),
            block, block, block, block, block, block, block, block,
            v((4, 2, PLANES, 128), F32), v((4, 2, PLANES, 128), F32),
            v((4, 128, 128), F32), v((4, 2, 128, 128), F32), v((128, 128), F32),
            v((2, 2, 288, 128), F32), v((2, 2, 288, 128), F32),
            v((2, CHUNK, 128), F32), v((2, 2, CHUNK, 128), F32),
            d((4,)), d((4,)), d((2,)), d((4,)), d((4,)),
            d((4, 4)), d((4, 4)), d((2, 4)), d((2, 4)),
        ],
        name="coupled",
        compiler_params=pltpu.CompilerParams(
            collective_id=0, has_side_effects=True, vmem_limit_bytes=60 * 1024 * 1024
        ),
    )(
        spectrum, weights, drift, courant,
        tile.reshape(1, PTS), cell.reshape(1, PTS), land.reshape(1, PTS),
        vel.reshape(PLANES, 128, 128), oland,
    )
    return e, o.reshape(2, LEV, 128, 128)


def solution(mesh):
    ocean = P(None, None, ("mp", "gx"), "gy")
    return jax.shard_map(
        step,
        mesh=mesh,
        in_specs=(
            P(None, ALL), P(), P(), P(), P(ALL, None), P(ALL), P(ALL),
            ocean, P(("mp", "gx"), "gy"),
        ),
        out_specs=(P(None, ALL), ocean),
        check_vma=False,
    )
```

```python
import jax
import jax.numpy as jnp
from jax import lax
from jax.experimental import pallas as pl
from jax.experimental.pallas import tpu as pltpu
from jax.sharding import PartitionSpec as P

ALL = ("mp", "gx", "gy")
F32 = jnp.float32
BF16 = jnp.bfloat16
MESH = pl.DeviceIdType.MESH

BINS = 1152
PTS = 128
LEV = 32
PLANES = 64
DEVS = 128
ROWS = 16
COLS = 8
PAD = 144
CHUNK = 72
MROWS = 384
STRIP = 128
UNROLL = 4


def near(a):
    return min(a, 4 - a)


OFFSETS = sorted(
    [
        (dx, dy, dz, dc)
        for dx in range(4)
        for dy in range(4)
        for dz in range(4)
        for dc in range(2)
        if (dx, dy, dz, dc) != (0, 0, 0, 0)
    ],
    key=lambda d: (-(near(d[0]) + near(d[1]) + near(d[2])), d),
)


def place(x, y, z, core):
    return (x // 2, z * 2 + x % 2, y * 2 + core)


def split(x):
    high = x.astype(BF16)
    low = (x - high.astype(F32)).astype(BF16)
    return high, low


def dot_nt(a, b):
    return lax.dot_general(a, b, (((1,), (1,)), ((), ())), preferred_element_type=F32)


def dot_tn(a, b):
    return lax.dot_general(a, b, (((0,), (0,)), ((), ())), preferred_element_type=F32)


def dot_nn(a, b):
    return jnp.dot(a, b, preferred_element_type=F32)


def kernel(
    spec_h, w_h, dw_h, cour_h, tile_h, cell_h, land_h, vel_h, oland_h,
    eout_v, oout_v,
    e_v, c_v, g_v, lin_v, w_v, dw_v, cx_v, cy_v, oa_v, ob_v, f_v, sea_v, ol_v, tri_v,
    q_v, rt_v, rs_v, cc_v, at_v, cour_v, tile_v, cell_v, land_v,
    s1, r1, s2, r2, s3, r3, s4, r4,
    rowp, rowr, colp, colr, hc_v,
    wrp, wrr, wcp, wcr,
    in_sem, w_sem, a_send, a_recv, h_send, h_recv, g_send, g_recv,
):
    mp, gx, gy = lax.axis_index("mp"), lax.axis_index("gx"), lax.axis_index("gy")
    row = mp * 8 + gx
    me = row * 8 + gy
    px, pz, py, pc = mp * 2 + gx % 2, gx // 2, gy // 2, gy % 2

    in_e = pltpu.make_async_copy(spec_h, e_v, in_sem.at[0])
    in_dw = pltpu.make_async_copy(dw_h, dw_v, in_sem.at[1])
    in_ol = pltpu.make_async_copy(oland_h, ol_v, in_sem.at[2])
    in_u = pltpu.make_async_copy(vel_h, oa_v.at[:, pl.ds(8, 128), :], in_sem.at[3])
    in_small = [
        pltpu.make_async_copy(src, dst, in_sem.at[4 + k])
        for k, (src, dst) in enumerate(
            ((tile_h, tile_v), (cell_h, cell_v), (land_h, land_v), (cour_h, cour_v))
        )
    ]
    for copy in in_small:
        copy.start()
    in_e.start()
    in_dw.start()
    in_u.start()
    in_ol.start()
    in_w = [pltpu.make_async_copy(w_h.at[m], w_v.at[m], w_sem.at[m]) for m in range(4)]
    for copy in in_w:
        copy.start()

    barrier = pltpu.get_barrier_semaphore()

    for dx, dy, dz, dc in OFFSETS:
        to = place((px + dx) % 4, (py + dy) % 4, (pz + dz) % 4, (pc + dc) % 2)
        pl.semaphore_signal(barrier, inc=1, device_id=to, device_id_type=MESH)

    lane = lax.broadcasted_iota(jnp.int32, (128, 128), 1)
    sub = lax.broadcasted_iota(jnp.int32, (128, 128), 0)

    def exchange_all(n, src, dst):
        for dx, dy, dz, dc in OFFSETS:
            to = place((px + dx) % 4, (py + dy) % 4, (pz + dz) % 4, (pc + dc) % 2)
            peer = (to[0] * 8 + to[1]) * 8 + to[2]
            pltpu.make_async_remote_copy(
                src_ref=src.at[peer], dst_ref=dst.at[me],
                send_sem=a_send.at[n], recv_sem=a_recv.at[n],
                device_id=to, device_id_type=MESH,
            ).start()
        dst[pl.ds(me, 1)] = src[pl.ds(me, 1)]

    def exchange_sent(n, src):
        block = src.at[pl.ds(0, DEVS - 1)]
        pltpu.make_async_copy(block, block, a_send.at[n]).wait()

    def exchange_come(n, dst):
        block = dst.at[pl.ds(0, DEVS - 1)]
        pltpu.make_async_copy(block, block, a_recv.at[n]).wait()

    up, down = (row + ROWS - 1) % ROWS, (row + 1) % ROWS
    left, right = (gy + COLS - 1) % COLS, (gy + 1) % COLS
    at_up, at_down = (up // 8, up % 8, gy), (down // 8, down % 8, gy)
    at_left, at_right = (mp, gx, left), (mp, gx, right)

    def halo_copies(rows_out, rows_in, cols_out, cols_in, ss, rs, n):
        def one(k, src, dst, to):
            return pltpu.make_async_remote_copy(
                src_ref=src, dst_ref=dst, send_sem=ss.at[n, k], recv_sem=rs.at[n, k],
                device_id=to, device_id_type=MESH,
            )

        return [
            one(0, rows_out.at[0], rows_in.at[1], at_up),
            one(1, rows_out.at[1], rows_in.at[0], at_down),
            one(2, cols_out, cols_in.at[1], at_left),
            one(3, cols_out, cols_in.at[0], at_right),
        ]

    ocean_halo = [
        halo_copies(rowp.at[n], rowr.at[n], colp.at[n], colr.at[n], h_send, h_recv, n)
        for n in range(4)
    ]
    wave_halo = [
        halo_copies(wrp.at[n], wrr.at[n], wcp.at[n], wcr.at[n], g_send, g_recv, n)
        for n in range(2)
    ]
    has_up = (row > 0).astype(F32)
    has_down = (row < ROWS - 1).astype(F32)
    has_left = (gy > 0).astype(F32)
    has_right = (gy < COLS - 1).astype(F32)

    for copy in in_small:
        copy.wait()
    tile_row = jnp.broadcast_to(tile_v[...], (128, 128))
    tile_col = tile_row.T
    before = jnp.where((tile_row == tile_col) & (sub < lane), 1.0, 0.0)
    rank = jnp.sum(before, axis=0, keepdims=True)
    for r in range(2):
        mine = (tile_row == sub) & (jnp.broadcast_to(rank, (128, 128)) == float(r))
        q_v[r] = jnp.where(mine, 1.0, 0.0).astype(BF16)

    def drift_out(dst):
        d = dot_nn(dw_v[...], c_v[...])
        extra = jnp.broadcast_to((cell_v[...] + 1).astype(F32), (64, 128))
        high, low = split(jnp.concatenate([d, extra], axis=0))
        for r in range(2):
            dst[:, r, :] = dot_nt(q_v[r], high) + dot_nt(q_v[r], low)

    in_e.wait()
    in_dw.wait()
    c_v[...] = e_v[...].astype(BF16)
    drift_out(s1)

    lane_s = lax.broadcasted_iota(jnp.int32, (STRIP, 128), 1)

    def pack_plane(n, p, s, x):
        if s == 0:
            rowp[n, 0, pl.ds(p, 1), :] = x[0:1]
        if s == 128 // STRIP - 1:
            rowp[n, 1, pl.ds(p, 1), :] = x[STRIP - 1 : STRIP]
        pltpu.store(
            colp.at[n, pl.ds(s * STRIP, STRIP), :],
            pltpu.roll(x, 2 * p + 1, 1),
            mask=(lane_s >> 1) == p,
        )

    def pack_first(p, carry):
        for s in range(128 // STRIP):
            pack_plane(0, p, s, oa_v[p, 8 + s * STRIP : 8 + (s + 1) * STRIP, :])
        return carry

    def pack_start():
        lax.fori_loop(0, PLANES, pack_first, 0, unroll=4)

    def linear(first, last):
        def one(i, carry):
            m, b = i // 3, i % 3
            rows = pl.ds(pl.multiple_of(b * MROWS, MROWS), MROWS)
            lin_v[m, rows, :] = dot_nn(w_v[m, rows, :], c_v[...])
            return carry

        lax.fori_loop(first, last, one, 0)

    in_w[0].wait()
    linear(0, 3)
    pl.semaphore_wait(barrier, DEVS - 1)
    exchange_all(0, s1, r1)
    in_u.wait()
    pack_start()
    for copy in ocean_halo[0]:
        copy.start()
    for b in range(BINS // 128):
        block = pl.ds(b * 128, 128)
        cx_v[block, :] = jnp.broadcast_to(cour_v[0:1, block], (128, 128)).T
        cy_v[block, :] = jnp.broadcast_to(cour_v[1:2, block], (128, 128)).T

    deep = lax.broadcasted_iota(jnp.int32, (256, 128), 0) & 127
    tall = lax.broadcasted_iota(jnp.int32, (256, 128), 1)
    tri_v[...] = jnp.where((deep - tall == 1) | (tall - deep == 1), 1.0, 0.0).astype(BF16)
    in_ol.wait()
    sea_v[...] = ol_v[...].astype(F32) * 0.2

    for copy in in_w[1:]:
        copy.wait()
    linear(3, 12)

    exchange_come(0, r1)

    def arrived(src):
        return jnp.concatenate([src[:, 0, :], src[:, 1, :]], axis=0)

    a = arrived(r1)
    at = a.T
    at_v[...] = at[0:PLANES] * 0.5
    cell_t = at[64:65, :].astype(jnp.int32) - 1
    wide = lax.broadcasted_iota(jnp.int32, (128, 256), 0)
    rt_v[...] = jnp.where(wide == jnp.broadcast_to(cell_t >> 7, (128, 256)), 1.0, 0.0).astype(BF16)
    cell_c = jnp.broadcast_to(a[:, 64:65], (256, 128)).astype(jnp.int32) - 1
    rs_v[...] = jnp.where(tall == (cell_c >> 7), 1.0, 0.0).astype(BF16)
    cc_v[...] = jnp.where(tall == (cell_c & 127), 1.0, 0.0).astype(BF16)

    def currents_out(ocean, dst):
        found = []
        for f in range(2):
            high, low = split(ocean[f * LEV, 8:136, :])
            x = dot_nn(rs_v[...], high) + dot_nn(rs_v[...], low)
            found.append(jnp.sum(x * cc_v[...].astype(F32), axis=1, keepdims=True))
        both = jnp.where(tall == 0, found[0], jnp.where(tall == 1, found[1], 0.0))
        dst[:, 0, :] = both[0:128]
        dst[:, 1, :] = both[128:256]

    currents_out(oa_v, s2)
    exchange_all(1, s2, r2)

    def forcing():
        def one(p, carry):
            high, low = split(jnp.broadcast_to(at_v[pl.ds(p, 1), :], (16, 256)))
            high = jnp.broadcast_to(high[0:1], (128, 256))
            low = jnp.broadcast_to(low[0:1], (128, 256))
            f_v[p] = dot_nn(rt_v[...] * high, cc_v[...]) + dot_nn(rt_v[...] * low, cc_v[...])
            return carry

        lax.fori_loop(0, PLANES, one, 0, unroll=16)

    def substep(n, src, dst, pack):
        for copy in ocean_halo[n]:
            copy.wait()
        src[:, 7, :] = rowr[n, 0] * has_up
        src[:, 136, :] = rowr[n, 1] * has_down
        even = (lane % 2) == 0
        hc_v[...] = jnp.where(
            even, colr[n, 0] * has_left, pltpu.roll(colr[n, 1], 126, 1) * has_right
        )

        brim = (lane == 0) | (lane == 127)

        def around(p):
            x = src[p, 8:136, :]
            high, low = split(x)
            across = dot_nn(jnp.concatenate([high, low], axis=1), tri_v[...])
            edge = jnp.where(brim, pltpu.roll(hc_v[...], (128 - 2 * p) % 128, 1), 0.0)
            return x, (src[p, 7:135, :] + src[p, 9:137, :]) + (x + edge) + across

        def one(l, carry):
            u, su = around(l)
            v, sv = around(LEV + l)
            un = sea_v[...] * (su + (0.5 * v + f_v[LEV + l]))
            vn = sea_v[...] * (sv - (0.5 * u + f_v[l]))
            if pack:
                dst[l, 8:136, :] = un
                dst[LEV + l, 8:136, :] = vn
            else:
                dst[l] = un
                dst[LEV + l] = vn
            if pack:
                for s in range(128 // STRIP):
                    rows = slice(s * STRIP, (s + 1) * STRIP)
                    pack_plane(n + 1, l, s, un[rows])
                    pack_plane(n + 1, LEV + l, s, vn[rows])
            return carry

        lax.fori_loop(0, LEV, one, 0, unroll=UNROLL)
        if pack:
            for copy in ocean_halo[n + 1]:
                copy.start()

    sea_row = land_v[...].astype(F32)
    lane_c = lax.broadcasted_iota(jnp.int32, (CHUNK, 128), 1)
    seg = lane_c // 32
    pos = lane_c % 32

    def grow(n, src):
        exchange_come(2 * n + 1 if n == 0 else 3, src)
        now = jnp.zeros((128, 128), F32)
        for r in range(2):
            high, low = split(src[:, r, :])
            now = now + dot_tn(high, q_v[r]) + dot_tn(low, q_v[r])
        cu, cv = now[0:1], now[1:2]

        def one(k, carry):
            first = jnp.zeros((CHUNK, 128), F32)
            last = jnp.zeros((CHUNK, 128), F32)
            cols = carry
            for q in range(4):
                rows = pl.ds(pl.multiple_of(288 * q + CHUNK * k, 8), CHUNK)
                g = sea_row * (
                    e_v[rows, :]
                    + 0.1 * lin_v[0, rows, :] * lin_v[1, rows, :]
                    + 0.1 * (cu * lin_v[2, rows, :] + cv * lin_v[3, rows, :])
                )
                g_v[rows, :] = g
                first = jnp.where(seg == q, pltpu.roll(g, 32 * q, 1) if q else g, first)
                last = jnp.where(seg == q, pltpu.roll(g, (32 * q + 32) % 128, 1) if q < 3 else g, last)
                group = 4 * q + k
                cols = jnp.where(pos // 2 == group, pltpu.roll(g, 2 * group + 1, 1), cols)
            part = pl.ds(pl.multiple_of(CHUNK * k, 8), CHUNK)
            wrp[n, 0, part, :] = first
            wrp[n, 1, part, :] = last
            return cols

        wcp[n] = lax.fori_loop(0, 4, one, jnp.zeros((CHUNK, 128), F32))
        for copy in wave_halo[n]:
            copy.start()

    def advect(n, dst):
        for copy in wave_halo[n]:
            copy.wait()
        cols = jnp.where(
            lane_c % 2 == 0,
            pltpu.roll(wcr[n, 0], 96, 1) * has_left,
            pltpu.roll(wcr[n, 1], 30, 1) * has_right,
        )
        flow_x = jnp.where(seg == 0, has_up, 1.0)
        flow_y = jnp.where(pos == 0, has_left, 1.0)

        def one(k, carry):
            part = pl.ds(pl.multiple_of(CHUNK * k, 8), CHUNK)
            above = wrr[n, 0, part, :] * has_up
            below = wrr[n, 1, part, :] * has_down
            for q in range(4):
                rows = pl.ds(pl.multiple_of(288 * q + CHUNK * k, 8), CHUNK)
                group = 4 * q + k
                g = g_v[rows, :]
                cx, cy = cx_v[rows, :], cy_v[rows, :]
                edge = pltpu.roll(cols, (128 - 2 * group) % 128, 1)
                g_down = jnp.where(
                    seg == 3, pltpu.roll(below, (96 - 32 * q) % 128, 1), pltpu.roll(g, 96, 1)
                )
                g_up = jnp.where(
                    seg == 0, pltpu.roll(above, (128 - 32 * q) % 128, 1), pltpu.roll(g, 32, 1)
                )
                g_right = jnp.where(pos == 31, edge, pltpu.roll(g, 127, 1))
                g_left = jnp.where(pos == 0, edge, pltpu.roll(g, 1, 1))
                px_, nx_ = jnp.maximum(cx, 0.0), jnp.minimum(cx, 0.0)
                py_, ny_ = jnp.maximum(cy, 0.0), jnp.minimum(cy, 0.0)
                out_x = px_ * g + nx_ * g_down
                in_x = flow_x * (px_ * g_up + nx_ * g)
                out_y = py_ * g + ny_ * g_right
                in_y = flow_y * (py_ * g_left + ny_ * g)
                dst[rows, :] = sea_row * (g - (out_x - in_x) - (out_y - in_y))
            return carry

        lax.fori_loop(0, 4, one, 0)

    forcing()
    substep(0, oa_v, ob_v, True)
    grow(0, r2)
    substep(1, ob_v, oa_v, True)
    currents_out(oa_v, s4)
    exchange_all(3, s4, r4)
    advect(0, e_v)
    c_v[...] = e_v[...].astype(BF16)
    drift_out(s3)
    exchange_all(2, s3, r3)
    linear(0, 12)
    grow(1, r4)
    exchange_come(2, r3)
    at_v[...] = arrived(r3).T[0:PLANES] * 0.5
    forcing()
    substep(2, oa_v, ob_v, True)
    advect(1, eout_v)
    substep(3, ob_v, oout_v, False)
    for n, src in enumerate((s1, s2, s3, s4)):
        exchange_sent(n, src)


def step(spectrum, weights, drift, courant, tile, cell, land, vel, oland):
    near_by = pl.BlockSpec(memory_space=pltpu.VMEM)
    far = pl.BlockSpec(memory_space=pltpu.HBM)
    v = pltpu.VMEM
    d = pltpu.SemaphoreType.DMA
    block = v((DEVS, 2, 128), F32)
    args = [
        pltpu.with_memory_space_constraint(x, pltpu.HBM)
        for x in (
            spectrum, weights, drift, courant,
            tile.reshape(1, PTS), cell.reshape(1, PTS), land.reshape(1, PTS),
            vel.reshape(PLANES, 128, 128), oland,
        )
    ]
    e, o = pl.pallas_call(
        kernel,
        out_shape=(
            jax.ShapeDtypeStruct((BINS, PTS), F32),
            jax.ShapeDtypeStruct((PLANES, 128, 128), F32),
        ),
        in_specs=[far] * 9,
        out_specs=(near_by, near_by),
        scratch_shapes=[
            v((BINS, 128), F32), v((BINS, 128), BF16), v((BINS, 128), F32),
            v((4, BINS, 128), F32), v((4, BINS, BINS), BF16), v((PLANES, BINS), BF16),
            v((BINS, 128), F32), v((BINS, 128), F32),
            v((PLANES, PAD, 128), F32), v((PLANES, PAD, 128), F32),
            v((PLANES, 128, 128), F32), v((128, 128), F32), v((128, 128), jnp.int32), v((256, 128), BF16),
            v((2, 128, 128), BF16), v((128, 256), BF16), v((256, 128), BF16),
            v((256, 128), BF16), v((PLANES, 256), F32),
            v((2, BINS), F32), v((1, PTS), jnp.int32), v((1, PTS), jnp.int32), v((1, PTS), jnp.int32),
            block, block, block, block, block, block, block, block,
            v((4, 2, PLANES, 128), F32), v((4, 2, PLANES, 128), F32),
            v((4, 128, 128), F32), v((4, 2, 128, 128), F32), v((128, 128), F32),
            v((2, 2, 288, 128), F32), v((2, 2, 288, 128), F32),
            v((2, CHUNK, 128), F32), v((2, 2, CHUNK, 128), F32),
            d((8,)), d((4,)), d((4,)), d((4,)),
            d((4, 4)), d((4, 4)), d((2, 4)), d((2, 4)),
        ],
        name="coupled",
        compiler_params=pltpu.CompilerParams(
            collective_id=0, has_side_effects=True, vmem_limit_bytes=42 * 1024 * 1024
        ),
    )(*args)
    return e, o.reshape(2, LEV, 128, 128)


def solution(mesh):
    ocean = P(None, None, ("mp", "gx"), "gy")
    return jax.shard_map(
        step,
        mesh=mesh,
        in_specs=(
            P(None, ALL), P(), P(), P(), P(ALL, None), P(ALL), P(ALL),
            ocean, P(("mp", "gx"), "gy"),
        ),
        out_specs=(P(None, ALL), ocean),
        check_vma=False,
    )
```

```python
import jax
import jax.numpy as jnp
from jax import lax
from jax.experimental import pallas as pl
from jax.experimental.pallas import tpu as pltpu
from jax.sharding import PartitionSpec as P

ALL = ("mp", "gx", "gy")
F32 = jnp.float32
BF16 = jnp.bfloat16
MESH = pl.DeviceIdType.MESH

BINS = 1152
PTS = 128
LEV = 32
PLANES = 64
DEVS = 128
ROWS = 16
COLS = 8
PAD = 144
CHUNK = 72
MROWS = 384
STRIP = 128
UNROLL = 4
FUSED = (0, 2)


def near(a):
    return min(a, 4 - a)


OFFSETS = sorted(
    [
        (dx, dy, dz, dc)
        for dx in range(4)
        for dy in range(4)
        for dz in range(4)
        for dc in range(2)
        if (dx, dy, dz, dc) != (0, 0, 0, 0)
    ],
    key=lambda d: (-(near(d[0]) + near(d[1]) + near(d[2])), d),
)


def place(x, y, z, core):
    return (x // 2, z * 2 + x % 2, y * 2 + core)


def split(x):
    high = x.astype(BF16)
    low = (x - high.astype(F32)).astype(BF16)
    return high, low


def dot_nt(a, b):
    return lax.dot_general(a, b, (((1,), (1,)), ((), ())), preferred_element_type=F32)


def dot_tn(a, b):
    return lax.dot_general(a, b, (((0,), (0,)), ((), ())), preferred_element_type=F32)


def dot_nn(a, b):
    return jnp.dot(a, b, preferred_element_type=F32)


def kernel(
    spec_h, w_h, dw_h, cour_h, tile_h, cell_h, land_h, vel_h, oland_h,
    eout_v, oout_v,
    e_v, c_v, g_v, lin_v, w_v, dw_v, cx_v, cy_v, oa_v, ob_v, f_v, sea_v, ol_v, tri_v,
    q_v, rt_v, rs_v, cc_v, at_v, cour_v, tile_v, cell_v, land_v,
    s1, r1, s2, r2, s3, r3, s4, r4,
    rowp, rowr, colp, colr, hc_v,
    wrp, wrr, wcp, wcr,
    in_sem, w_sem, a_send, a_recv, h_send, h_recv, g_send, g_recv,
):
    mp, gx, gy = lax.axis_index("mp"), lax.axis_index("gx"), lax.axis_index("gy")
    row = mp * 8 + gx
    me = row * 8 + gy
    px, pz, py, pc = mp * 2 + gx % 2, gx // 2, gy // 2, gy % 2

    in_e = pltpu.make_async_copy(spec_h, e_v, in_sem.at[0])
    in_dw = pltpu.make_async_copy(dw_h, dw_v, in_sem.at[1])
    in_ol = pltpu.make_async_copy(oland_h, ol_v, in_sem.at[2])
    in_u = pltpu.make_async_copy(vel_h, oa_v.at[:, pl.ds(8, 128), :], in_sem.at[3])
    in_small = [
        pltpu.make_async_copy(src, dst, in_sem.at[4 + k])
        for k, (src, dst) in enumerate(
            ((tile_h, tile_v), (cell_h, cell_v), (land_h, land_v), (cour_h, cour_v))
        )
    ]
    for copy in in_small:
        copy.start()
    in_e.start()
    in_dw.start()
    in_u.start()
    in_ol.start()
    in_w = [pltpu.make_async_copy(w_h.at[m], w_v.at[m], w_sem.at[m]) for m in range(4)]
    for copy in in_w:
        copy.start()

    barrier = pltpu.get_barrier_semaphore()

    for dx, dy, dz, dc in OFFSETS:
        to = place((px + dx) % 4, (py + dy) % 4, (pz + dz) % 4, (pc + dc) % 2)
        pl.semaphore_signal(barrier, inc=1, device_id=to, device_id_type=MESH)

    lane = lax.broadcasted_iota(jnp.int32, (128, 128), 1)
    sub = lax.broadcasted_iota(jnp.int32, (128, 128), 0)

    def exchange_all(n, src, dst):
        for dx, dy, dz, dc in OFFSETS:
            to = place((px + dx) % 4, (py + dy) % 4, (pz + dz) % 4, (pc + dc) % 2)
            peer = (to[0] * 8 + to[1]) * 8 + to[2]
            pltpu.make_async_remote_copy(
                src_ref=src.at[peer], dst_ref=dst.at[me],
                send_sem=a_send.at[n], recv_sem=a_recv.at[n],
                device_id=to, device_id_type=MESH,
            ).start()
        dst[pl.ds(me, 1)] = src[pl.ds(me, 1)]

    def exchange_sent(n, src):
        block = src.at[pl.ds(0, DEVS - 1)]
        pltpu.make_async_copy(block, block, a_send.at[n]).wait()

    def exchange_come(n, dst):
        block = dst.at[pl.ds(0, DEVS - 1)]
        pltpu.make_async_copy(block, block, a_recv.at[n]).wait()

    up, down = (row + ROWS - 1) % ROWS, (row + 1) % ROWS
    left, right = (gy + COLS - 1) % COLS, (gy + 1) % COLS
    at_up, at_down = (up // 8, up % 8, gy), (down // 8, down % 8, gy)
    at_left, at_right = (mp, gx, left), (mp, gx, right)

    def halo_copies(rows_out, rows_in, cols_out, cols_in, ss, rs, n):
        def one(k, src, dst, to):
            return pltpu.make_async_remote_copy(
                src_ref=src, dst_ref=dst, send_sem=ss.at[n, k], recv_sem=rs.at[n, k],
                device_id=to, device_id_type=MESH,
            )

        return [
            one(0, rows_out.at[0], rows_in.at[1], at_up),
            one(1, rows_out.at[1], rows_in.at[0], at_down),
            one(2, cols_out, cols_in.at[1], at_left),
            one(3, cols_out, cols_in.at[0], at_right),
        ]

    ocean_halo = [
        halo_copies(rowp.at[n], rowr.at[n], colp.at[n], colr.at[n], h_send, h_recv, n)
        for n in range(4)
    ]
    wave_halo = [
        halo_copies(wrp.at[n], wrr.at[n], wcp.at[n], wcr.at[n], g_send, g_recv, n)
        for n in range(2)
    ]
    has_up = (row > 0).astype(F32)
    has_down = (row < ROWS - 1).astype(F32)
    has_left = (gy > 0).astype(F32)
    has_right = (gy < COLS - 1).astype(F32)

    for copy in in_small:
        copy.wait()
    tile_row = jnp.broadcast_to(tile_v[...], (128, 128))
    tile_col = tile_row.T
    before = jnp.where((tile_row == tile_col) & (sub < lane), 1.0, 0.0)
    rank = jnp.sum(before, axis=0, keepdims=True)
    for r in range(2):
        mine = (tile_row == sub) & (jnp.broadcast_to(rank, (128, 128)) == float(r))
        q_v[r] = jnp.where(mine, 1.0, 0.0).astype(BF16)

    def drift_out(dst):
        d = dot_nn(dw_v[...], c_v[...])
        extra = jnp.broadcast_to((cell_v[...] + 1).astype(F32), (64, 128))
        high, low = split(jnp.concatenate([d, extra], axis=0))
        for r in range(2):
            dst[:, r, :] = dot_nt(q_v[r], high) + dot_nt(q_v[r], low)

    in_e.wait()
    in_dw.wait()
    c_v[...] = e_v[...].astype(BF16)
    drift_out(s1)

    lane_s = lax.broadcasted_iota(jnp.int32, (STRIP, 128), 1)

    def pack_plane(n, p, s, x):
        if s == 0:
            rowp[n, 0, pl.ds(p, 1), :] = x[0:1]
        if s == 128 // STRIP - 1:
            rowp[n, 1, pl.ds(p, 1), :] = x[STRIP - 1 : STRIP]
        pltpu.store(
            colp.at[n, pl.ds(s * STRIP, STRIP), :],
            pltpu.roll(x, 2 * p + 1, 1),
            mask=(lane_s >> 1) == p,
        )

    def pack_first(p, carry):
        for s in range(128 // STRIP):
            pack_plane(0, p, s, oa_v[p, 8 + s * STRIP : 8 + (s + 1) * STRIP, :])
        return carry

    def pack_start():
        lax.fori_loop(0, PLANES, pack_first, 0, unroll=4)

    def linear(first, last):
        def one(i, carry):
            m, b = i // 3, i % 3
            rows = pl.ds(pl.multiple_of(b * MROWS, MROWS), MROWS)
            lin_v[m, rows, :] = dot_nn(w_v[m, rows, :], c_v[...])
            return carry

        lax.fori_loop(first, last, one, 0)

    in_w[0].wait()
    linear(0, 3)
    pl.semaphore_wait(barrier, DEVS - 1)
    exchange_all(0, s1, r1)
    in_u.wait()
    pack_start()
    for copy in ocean_halo[0]:
        copy.start()
    for b in range(BINS // 128):
        block = pl.ds(b * 128, 128)
        cx_v[block, :] = jnp.broadcast_to(cour_v[0:1, block], (128, 128)).T
        cy_v[block, :] = jnp.broadcast_to(cour_v[1:2, block], (128, 128)).T

    deep = lax.broadcasted_iota(jnp.int32, (256, 128), 0) & 127
    tall = lax.broadcasted_iota(jnp.int32, (256, 128), 1)
    tri_v[...] = jnp.where((deep - tall == 1) | (tall - deep == 1), 1.0, 0.0).astype(BF16)
    in_ol.wait()
    sea_v[...] = ol_v[...].astype(F32) * 0.2

    for copy in in_w[1:]:
        copy.wait()
    linear(3, 12)

    exchange_come(0, r1)

    def arrived(src):
        return jnp.concatenate([src[:, 0, :], src[:, 1, :]], axis=0)

    a = arrived(r1)
    at = a.T
    at_v[...] = at[0:PLANES] * 0.5
    cell_t = at[64:65, :].astype(jnp.int32) - 1
    wide = lax.broadcasted_iota(jnp.int32, (128, 256), 0)
    rt_v[...] = jnp.where(wide == jnp.broadcast_to(cell_t >> 7, (128, 256)), 1.0, 0.0).astype(BF16)
    cell_c = jnp.broadcast_to(a[:, 64:65], (256, 128)).astype(jnp.int32) - 1
    rs_v[...] = jnp.where(tall == (cell_c >> 7), 1.0, 0.0).astype(BF16)
    cc_v[...] = jnp.where(tall == (cell_c & 127), 1.0, 0.0).astype(BF16)

    def currents_out(ocean, dst):
        found = []
        for f in range(2):
            high, low = split(ocean[f * LEV, 8:136, :])
            x = dot_nn(rs_v[...], high) + dot_nn(rs_v[...], low)
            found.append(jnp.sum(x * cc_v[...].astype(F32), axis=1, keepdims=True))
        both = jnp.where(tall == 0, found[0], jnp.where(tall == 1, found[1], 0.0))
        dst[:, 0, :] = both[0:128]
        dst[:, 1, :] = both[128:256]

    currents_out(oa_v, s2)
    exchange_all(1, s2, r2)

    def force(p):
        high, low = split(jnp.broadcast_to(at_v[pl.ds(p, 1), :], (16, 256)))
        high = jnp.broadcast_to(high[0:1], (128, 256))
        low = jnp.broadcast_to(low[0:1], (128, 256))
        return dot_nn(rt_v[...] * high, cc_v[...]) + dot_nn(rt_v[...] * low, cc_v[...])

    def forcing():
        def one(p, carry):
            f_v[p] = force(p)
            return carry

        lax.fori_loop(0, PLANES, one, 0, unroll=16)

    def substep(n, src, dst, pack):
        for copy in ocean_halo[n]:
            copy.wait()
        src[:, 7, :] = rowr[n, 0] * has_up
        src[:, 136, :] = rowr[n, 1] * has_down
        even = (lane % 2) == 0
        hc_v[...] = jnp.where(
            even, colr[n, 0] * has_left, pltpu.roll(colr[n, 1], 126, 1) * has_right
        )

        brim = (lane == 0) | (lane == 127)

        def around(p):
            x = src[p, 8:136, :]
            high, low = split(x)
            across = dot_nn(jnp.concatenate([high, low], axis=1), tri_v[...])
            edge = jnp.where(brim, pltpu.roll(hc_v[...], (128 - 2 * p) % 128, 1), 0.0)
            return x, (src[p, 7:135, :] + src[p, 9:137, :]) + (x + edge) + across

        def one(l, carry):
            u, su = around(l)
            v, sv = around(LEV + l)
            if n in FUSED:
                fe, fn = force(l), force(LEV + l)
                f_v[l] = fe
                f_v[LEV + l] = fn
            else:
                fe, fn = f_v[l], f_v[LEV + l]
            un = sea_v[...] * (su + (0.5 * v + fn))
            vn = sea_v[...] * (sv - (0.5 * u + fe))
            if pack:
                dst[l, 8:136, :] = un
                dst[LEV + l, 8:136, :] = vn
            else:
                dst[l] = un
                dst[LEV + l] = vn
            if pack:
                for s in range(128 // STRIP):
                    rows = slice(s * STRIP, (s + 1) * STRIP)
                    pack_plane(n + 1, l, s, un[rows])
                    pack_plane(n + 1, LEV + l, s, vn[rows])
            return carry

        lax.fori_loop(0, LEV, one, 0, unroll=UNROLL)
        if pack:
            for copy in ocean_halo[n + 1]:
                copy.start()

    sea_row = land_v[...].astype(F32)
    lane_c = lax.broadcasted_iota(jnp.int32, (CHUNK, 128), 1)
    seg = lane_c // 32
    pos = lane_c % 32

    def grow(n, src):
        exchange_come(2 * n + 1 if n == 0 else 3, src)
        now = jnp.zeros((128, 128), F32)
        for r in range(2):
            high, low = split(src[:, r, :])
            now = now + dot_tn(high, q_v[r]) + dot_tn(low, q_v[r])
        cu, cv = now[0:1], now[1:2]

        def one(k, carry):
            first = jnp.zeros((CHUNK, 128), F32)
            last = jnp.zeros((CHUNK, 128), F32)
            cols = carry
            for q in range(4):
                rows = pl.ds(pl.multiple_of(288 * q + CHUNK * k, 8), CHUNK)
                g = sea_row * (
                    e_v[rows, :]
                    + 0.1 * lin_v[0, rows, :] * lin_v[1, rows, :]
                    + 0.1 * (cu * lin_v[2, rows, :] + cv * lin_v[3, rows, :])
                )
                g_v[rows, :] = g
                first = jnp.where(seg == q, pltpu.roll(g, 32 * q, 1) if q else g, first)
                last = jnp.where(seg == q, pltpu.roll(g, (32 * q + 32) % 128, 1) if q < 3 else g, last)
                group = 4 * q + k
                cols = jnp.where(pos // 2 == group, pltpu.roll(g, 2 * group + 1, 1), cols)
            part = pl.ds(pl.multiple_of(CHUNK * k, 8), CHUNK)
            wrp[n, 0, part, :] = first
            wrp[n, 1, part, :] = last
            return cols

        wcp[n] = lax.fori_loop(0, 4, one, jnp.zeros((CHUNK, 128), F32))
        for copy in wave_halo[n]:
            copy.start()

    def advect(n, dst):
        for copy in wave_halo[n]:
            copy.wait()
        cols = jnp.where(
            lane_c % 2 == 0,
            pltpu.roll(wcr[n, 0], 96, 1) * has_left,
            pltpu.roll(wcr[n, 1], 30, 1) * has_right,
        )
        flow_x = jnp.where(seg == 0, has_up, 1.0)
        flow_y = jnp.where(pos == 0, has_left, 1.0)

        def one(k, carry):
            part = pl.ds(pl.multiple_of(CHUNK * k, 8), CHUNK)
            above = wrr[n, 0, part, :] * has_up
            below = wrr[n, 1, part, :] * has_down
            for q in range(4):
                rows = pl.ds(pl.multiple_of(288 * q + CHUNK * k, 8), CHUNK)
                group = 4 * q + k
                g = g_v[rows, :]
                cx, cy = cx_v[rows, :], cy_v[rows, :]
                edge = pltpu.roll(cols, (128 - 2 * group) % 128, 1)
                g_down = jnp.where(
                    seg == 3, pltpu.roll(below, (96 - 32 * q) % 128, 1), pltpu.roll(g, 96, 1)
                )
                g_up = jnp.where(
                    seg == 0, pltpu.roll(above, (128 - 32 * q) % 128, 1), pltpu.roll(g, 32, 1)
                )
                g_right = jnp.where(pos == 31, edge, pltpu.roll(g, 127, 1))
                g_left = jnp.where(pos == 0, edge, pltpu.roll(g, 1, 1))
                px_, nx_ = jnp.maximum(cx, 0.0), jnp.minimum(cx, 0.0)
                py_, ny_ = jnp.maximum(cy, 0.0), jnp.minimum(cy, 0.0)
                out_x = px_ * g + nx_ * g_down
                in_x = flow_x * (px_ * g_up + nx_ * g)
                out_y = py_ * g + ny_ * g_right
                in_y = flow_y * (py_ * g_left + ny_ * g)
                dst[rows, :] = sea_row * (g - (out_x - in_x) - (out_y - in_y))
            return carry

        lax.fori_loop(0, 4, one, 0)

    substep(0, oa_v, ob_v, True)
    grow(0, r2)
    substep(1, ob_v, oa_v, True)
    currents_out(oa_v, s4)
    exchange_all(3, s4, r4)
    advect(0, e_v)
    c_v[...] = e_v[...].astype(BF16)
    drift_out(s3)
    exchange_all(2, s3, r3)
    linear(0, 12)
    grow(1, r4)
    exchange_come(2, r3)
    at_v[...] = arrived(r3).T[0:PLANES] * 0.5
    substep(2, oa_v, ob_v, True)
    advect(1, eout_v)
    substep(3, ob_v, oout_v, False)
    for n, src in enumerate((s1, s2, s3, s4)):
        exchange_sent(n, src)


def step(spectrum, weights, drift, courant, tile, cell, land, vel, oland):
    near_by = pl.BlockSpec(memory_space=pltpu.VMEM)
    far = pl.BlockSpec(memory_space=pltpu.HBM)
    v = pltpu.VMEM
    d = pltpu.SemaphoreType.DMA
    block = v((DEVS, 2, 128), F32)
    args = [
        pltpu.with_memory_space_constraint(x, pltpu.HBM)
        for x in (
            spectrum, weights, drift, courant,
            tile.reshape(1, PTS), cell.reshape(1, PTS), land.reshape(1, PTS),
            vel.reshape(PLANES, 128, 128), oland,
        )
    ]
    e, o = pl.pallas_call(
        kernel,
        out_shape=(
            jax.ShapeDtypeStruct((BINS, PTS), F32),
            jax.ShapeDtypeStruct((PLANES, 128, 128), F32),
        ),
        in_specs=[far] * 9,
        out_specs=(near_by, near_by),
        scratch_shapes=[
            v((BINS, 128), F32), v((BINS, 128), BF16), v((BINS, 128), F32),
            v((4, BINS, 128), F32), v((4, BINS, BINS), BF16), v((PLANES, BINS), BF16),
            v((BINS, 128), F32), v((BINS, 128), F32),
            v((PLANES, PAD, 128), F32), v((PLANES, PAD, 128), F32),
            v((PLANES, 128, 128), F32), v((128, 128), F32), v((128, 128), jnp.int32), v((256, 128), BF16),
            v((2, 128, 128), BF16), v((128, 256), BF16), v((256, 128), BF16),
            v((256, 128), BF16), v((PLANES, 256), F32),
            v((2, BINS), F32), v((1, PTS), jnp.int32), v((1, PTS), jnp.int32), v((1, PTS), jnp.int32),
            block, block, block, block, block, block, block, block,
            v((4, 2, PLANES, 128), F32), v((4, 2, PLANES, 128), F32),
            v((4, 128, 128), F32), v((4, 2, 128, 128), F32), v((128, 128), F32),
            v((2, 2, 288, 128), F32), v((2, 2, 288, 128), F32),
            v((2, CHUNK, 128), F32), v((2, 2, CHUNK, 128), F32),
            d((8,)), d((4,)), d((4,)), d((4,)),
            d((4, 4)), d((4, 4)), d((2, 4)), d((2, 4)),
        ],
        name="coupled",
        compiler_params=pltpu.CompilerParams(
            collective_id=0, has_side_effects=True, vmem_limit_bytes=42 * 1024 * 1024
        ),
    )(*args)
    return e, o.reshape(2, LEV, 128, 128)


def solution(mesh):
    ocean = P(None, None, ("mp", "gx"), "gy")
    return jax.shard_map(
        step,
        mesh=mesh,
        in_specs=(
            P(None, ALL), P(), P(), P(), P(ALL, None), P(ALL), P(ALL),
            ocean, P(("mp", "gx"), "gy"),
        ),
        out_specs=(P(None, ALL), ocean),
        check_vma=False,
    )
```

```python
import jax
import jax.numpy as jnp
from jax import lax
from jax.experimental import pallas as pl
from jax.experimental.pallas import tpu as pltpu
from jax.sharding import PartitionSpec as P

ALL = ("mp", "gx", "gy")
F32 = jnp.float32
BF16 = jnp.bfloat16
MESH = pl.DeviceIdType.MESH

BINS = 1152
PTS = 128
LEV = 32
PLANES = 64
DEVS = 128
ROWS = 16
COLS = 8
PAD = 144
CHUNK = 72
MROWS = 384
STRIP = 128
UNROLL = 4
FUSED = (0, 2)


def near(a):
    return min(a, 4 - a)


OFFSETS = sorted(
    [
        (dx, dy, dz, dc)
        for dx in range(4)
        for dy in range(4)
        for dz in range(4)
        for dc in range(2)
        if (dx, dy, dz, dc) != (0, 0, 0, 0)
    ],
    key=lambda d: (-(near(d[0]) + near(d[1]) + near(d[2])), d),
)


def place(x, y, z, core):
    return (x // 2, z * 2 + x % 2, y * 2 + core)


def split(x):
    high = x.astype(BF16)
    low = (x - high.astype(F32)).astype(BF16)
    return high, low


def dot_nt(a, b):
    return lax.dot_general(a, b, (((1,), (1,)), ((), ())), preferred_element_type=F32)


def dot_tn(a, b):
    return lax.dot_general(a, b, (((0,), (0,)), ((), ())), preferred_element_type=F32)


def dot_nn(a, b):
    return jnp.dot(a, b, preferred_element_type=F32)


def kernel(
    spec_h, w_h, dw_h, cour_h, tile_h, cell_h, land_h, vel_h, oland_h,
    eout_v, oout_v,
    e_v, c_v, g_v, lin_v, w_v, dw_v, cx_v, cy_v, oa_v, ob_v, f_v, sea_v, ol_v, tri_v,
    q_v, rt_v, rs_v, cc_v, at_v, cour_v, tile_v, cell_v, land_v,
    s1, r1, s2, r2, s3, r3, s4, r4,
    rowp, rowr, colp, colr, hc_v,
    wrp, wrr, wcp, wcr,
    in_sem, w_sem, a_send, a_recv, h_send, h_recv, g_send, g_recv,
):
    mp, gx, gy = lax.axis_index("mp"), lax.axis_index("gx"), lax.axis_index("gy")
    row = mp * 8 + gx
    me = row * 8 + gy
    px, pz, py, pc = mp * 2 + gx % 2, gx // 2, gy // 2, gy % 2

    in_e = pltpu.make_async_copy(spec_h, e_v, in_sem.at[0])
    in_dw = pltpu.make_async_copy(dw_h, dw_v, in_sem.at[1])
    in_ol = pltpu.make_async_copy(oland_h, ol_v, in_sem.at[2])
    in_u = pltpu.make_async_copy(vel_h, oa_v.at[:, pl.ds(8, 128), :], in_sem.at[3])
    in_small = [
        pltpu.make_async_copy(src, dst, in_sem.at[4 + k])
        for k, (src, dst) in enumerate(
            ((tile_h, tile_v), (cell_h, cell_v), (land_h, land_v), (cour_h, cour_v))
        )
    ]
    for copy in in_small:
        copy.start()
    in_e.start()
    in_dw.start()
    in_u.start()
    in_ol.start()
    in_w = [pltpu.make_async_copy(w_h.at[m], w_v.at[m], w_sem.at[m]) for m in range(4)]
    for copy in in_w:
        copy.start()

    barrier = pltpu.get_barrier_semaphore()

    for dx, dy, dz, dc in OFFSETS:
        to = place((px + dx) % 4, (py + dy) % 4, (pz + dz) % 4, (pc + dc) % 2)
        pl.semaphore_signal(barrier, inc=1, device_id=to, device_id_type=MESH)

    lane = lax.broadcasted_iota(jnp.int32, (128, 128), 1)
    sub = lax.broadcasted_iota(jnp.int32, (128, 128), 0)

    def exchange_all(n, src, dst):
        for dx, dy, dz, dc in OFFSETS:
            to = place((px + dx) % 4, (py + dy) % 4, (pz + dz) % 4, (pc + dc) % 2)
            peer = (to[0] * 8 + to[1]) * 8 + to[2]
            pltpu.make_async_remote_copy(
                src_ref=src.at[peer], dst_ref=dst.at[me],
                send_sem=a_send.at[n], recv_sem=a_recv.at[n],
                device_id=to, device_id_type=MESH,
            ).start()
        dst[pl.ds(me, 1)] = src[pl.ds(me, 1)]

    def exchange_sent(n, src):
        block = src.at[pl.ds(0, DEVS - 1)]
        pltpu.make_async_copy(block, block, a_send.at[n]).wait()

    def exchange_come(n, dst):
        block = dst.at[pl.ds(0, DEVS - 1)]
        pltpu.make_async_copy(block, block, a_recv.at[n]).wait()

    up, down = (row + ROWS - 1) % ROWS, (row + 1) % ROWS
    left, right = (gy + COLS - 1) % COLS, (gy + 1) % COLS
    at_up, at_down = (up // 8, up % 8, gy), (down // 8, down % 8, gy)
    at_left, at_right = (mp, gx, left), (mp, gx, right)

    def halo_copies(rows_out, rows_in, cols_out, cols_in, ss, rs, n):
        def one(k, src, dst, to):
            return pltpu.make_async_remote_copy(
                src_ref=src, dst_ref=dst, send_sem=ss.at[n, k], recv_sem=rs.at[n, k],
                device_id=to, device_id_type=MESH,
            )

        return [
            one(0, rows_out.at[0], rows_in.at[1], at_up),
            one(1, rows_out.at[1], rows_in.at[0], at_down),
            one(2, cols_out, cols_in.at[1], at_left),
            one(3, cols_out, cols_in.at[0], at_right),
        ]

    ocean_halo = [
        halo_copies(rowp.at[n], rowr.at[n], colp.at[n], colr.at[n], h_send, h_recv, n)
        for n in range(4)
    ]
    wave_halo = [
        halo_copies(wrp.at[n], wrr.at[n], wcp.at[n], wcr.at[n], g_send, g_recv, n)
        for n in range(2)
    ]
    has_up = (row > 0).astype(F32)
    has_down = (row < ROWS - 1).astype(F32)
    has_left = (gy > 0).astype(F32)
    has_right = (gy < COLS - 1).astype(F32)

    for copy in in_small:
        copy.wait()
    tile_row = jnp.broadcast_to(tile_v[...], (128, 128))
    tile_col = tile_row.T
    before = jnp.where((tile_row == tile_col) & (sub < lane), 1.0, 0.0)
    rank = jnp.sum(before, axis=0, keepdims=True)
    for r in range(2):
        mine = (tile_row == sub) & (jnp.broadcast_to(rank, (128, 128)) == float(r))
        q_v[r] = jnp.where(mine, 1.0, 0.0).astype(BF16)

    def drift_out(dst):
        d = dot_nn(dw_v[...], c_v[...])
        extra = jnp.broadcast_to((cell_v[...] + 1).astype(F32), (64, 128))
        high, low = split(jnp.concatenate([d, extra], axis=0))
        for r in range(2):
            dst[:, r, :] = dot_nt(q_v[r], high) + dot_nt(q_v[r], low)

    in_e.wait()
    in_dw.wait()
    c_v[...] = e_v[...].astype(BF16)
    drift_out(s1)

    lane_s = lax.broadcasted_iota(jnp.int32, (STRIP, 128), 1)

    def pack_plane(n, p, s, x):
        if s == 0:
            rowp[n, 0, pl.ds(p, 1), :] = x[0:1]
        if s == 128 // STRIP - 1:
            rowp[n, 1, pl.ds(p, 1), :] = x[STRIP - 1 : STRIP]
        pltpu.store(
            colp.at[n, pl.ds(s * STRIP, STRIP), :],
            pltpu.roll(x, 2 * p + 1, 1),
            mask=(lane_s >> 1) == p,
        )

    def pack_first(p, carry):
        for s in range(128 // STRIP):
            pack_plane(0, p, s, oa_v[p, 8 + s * STRIP : 8 + (s + 1) * STRIP, :])
        return carry

    def pack_start():
        lax.fori_loop(0, PLANES, pack_first, 0, unroll=4)

    def linear(first, last):
        def one(i, carry):
            m, b = i // 3, i % 3
            rows = pl.ds(pl.multiple_of(b * MROWS, MROWS), MROWS)
            lin_v[m, rows, :] = dot_nn(w_v[m, rows, :], c_v[...])
            return carry

        lax.fori_loop(first, last, one, 0)

    pl.semaphore_wait(barrier, DEVS - 1)
    exchange_all(0, s1, r1)
    in_u.wait()
    pack_start()
    for copy in ocean_halo[0]:
        copy.start()
    for b in range(BINS // 128):
        block = pl.ds(b * 128, 128)
        cx_v[block, :] = jnp.broadcast_to(cour_v[0:1, block], (128, 128)).T
        cy_v[block, :] = jnp.broadcast_to(cour_v[1:2, block], (128, 128)).T

    deep = lax.broadcasted_iota(jnp.int32, (256, 128), 0) & 127
    tall = lax.broadcasted_iota(jnp.int32, (256, 128), 1)
    tri_v[...] = jnp.where((deep - tall == 1) | (tall - deep == 1), 1.0, 0.0).astype(BF16)
    in_ol.wait()
    sea_v[...] = ol_v[...].astype(F32) * 0.2

    for copy in in_w:
        copy.wait()
    linear(0, 9)

    exchange_come(0, r1)

    def arrived(src):
        return jnp.concatenate([src[:, 0, :], src[:, 1, :]], axis=0)

    a = arrived(r1)
    at = a.T
    at_v[...] = at[0:PLANES] * 0.5
    cell_t = at[64:65, :].astype(jnp.int32) - 1
    wide = lax.broadcasted_iota(jnp.int32, (128, 256), 0)
    rt_v[...] = jnp.where(wide == jnp.broadcast_to(cell_t >> 7, (128, 256)), 1.0, 0.0).astype(BF16)
    cell_c = jnp.broadcast_to(a[:, 64:65], (256, 128)).astype(jnp.int32) - 1
    rs_v[...] = jnp.where(tall == (cell_c >> 7), 1.0, 0.0).astype(BF16)
    cc_v[...] = jnp.where(tall == (cell_c & 127), 1.0, 0.0).astype(BF16)

    def currents_out(ocean, dst):
        found = []
        for f in range(2):
            high, low = split(ocean[f * LEV, 8:136, :])
            x = dot_nn(rs_v[...], high) + dot_nn(rs_v[...], low)
            found.append(jnp.sum(x * cc_v[...].astype(F32), axis=1, keepdims=True))
        both = jnp.where(tall == 0, found[0], jnp.where(tall == 1, found[1], 0.0))
        dst[:, 0, :] = both[0:128]
        dst[:, 1, :] = both[128:256]

    currents_out(oa_v, s2)
    exchange_all(1, s2, r2)
    linear(9, 12)

    def force(p):
        high, low = split(jnp.broadcast_to(at_v[pl.ds(p, 1), :], (16, 256)))
        high = jnp.broadcast_to(high[0:1], (128, 256))
        low = jnp.broadcast_to(low[0:1], (128, 256))
        return dot_nn(rt_v[...] * high, cc_v[...]) + dot_nn(rt_v[...] * low, cc_v[...])

    def forcing():
        def one(p, carry):
            f_v[p] = force(p)
            return carry

        lax.fori_loop(0, PLANES, one, 0, unroll=16)

    def substep(n, src, dst, pack):
        for copy in ocean_halo[n]:
            copy.wait()
        src[:, 7, :] = rowr[n, 0] * has_up
        src[:, 136, :] = rowr[n, 1] * has_down
        even = (lane % 2) == 0
        hc_v[...] = jnp.where(
            even, colr[n, 0] * has_left, pltpu.roll(colr[n, 1], 126, 1) * has_right
        )

        brim = (lane == 0) | (lane == 127)

        def around(p):
            x = src[p, 8:136, :]
            high, low = split(x)
            across = dot_nn(jnp.concatenate([high, low], axis=1), tri_v[...])
            edge = jnp.where(brim, pltpu.roll(hc_v[...], (128 - 2 * p) % 128, 1), 0.0)
            return x, (src[p, 7:135, :] + src[p, 9:137, :]) + (x + edge) + across

        def one(l, carry):
            u, su = around(l)
            v, sv = around(LEV + l)
            if n in FUSED:
                fe, fn = force(l), force(LEV + l)
                f_v[l] = fe
                f_v[LEV + l] = fn
            else:
                fe, fn = f_v[l], f_v[LEV + l]
            un = sea_v[...] * (su + (0.5 * v + fn))
            vn = sea_v[...] * (sv - (0.5 * u + fe))
            if pack:
                dst[l, 8:136, :] = un
                dst[LEV + l, 8:136, :] = vn
            else:
                dst[l] = un
                dst[LEV + l] = vn
            if pack:
                for s in range(128 // STRIP):
                    rows = slice(s * STRIP, (s + 1) * STRIP)
                    pack_plane(n + 1, l, s, un[rows])
                    pack_plane(n + 1, LEV + l, s, vn[rows])
            return carry

        lax.fori_loop(0, LEV, one, 0, unroll=UNROLL)
        if pack:
            for copy in ocean_halo[n + 1]:
                copy.start()

    sea_row = land_v[...].astype(F32)
    lane_c = lax.broadcasted_iota(jnp.int32, (CHUNK, 128), 1)
    seg = lane_c // 32
    pos = lane_c % 32

    def grow(n, src):
        exchange_come(2 * n + 1 if n == 0 else 3, src)
        now = jnp.zeros((128, 128), F32)
        for r in range(2):
            high, low = split(src[:, r, :])
            now = now + dot_tn(high, q_v[r]) + dot_tn(low, q_v[r])
        cu, cv = now[0:1], now[1:2]

        def one(k, carry):
            first = jnp.zeros((CHUNK, 128), F32)
            last = jnp.zeros((CHUNK, 128), F32)
            cols = carry
            for q in range(4):
                rows = pl.ds(pl.multiple_of(288 * q + CHUNK * k, 8), CHUNK)
                g = sea_row * (
                    e_v[rows, :]
                    + 0.1 * lin_v[0, rows, :] * lin_v[1, rows, :]
                    + 0.1 * (cu * lin_v[2, rows, :] + cv * lin_v[3, rows, :])
                )
                g_v[rows, :] = g
                first = jnp.where(seg == q, pltpu.roll(g, 32 * q, 1) if q else g, first)
                last = jnp.where(seg == q, pltpu.roll(g, (32 * q + 32) % 128, 1) if q < 3 else g, last)
                group = 4 * q + k
                cols = jnp.where(pos // 2 == group, pltpu.roll(g, 2 * group + 1, 1), cols)
            part = pl.ds(pl.multiple_of(CHUNK * k, 8), CHUNK)
            wrp[n, 0, part, :] = first
            wrp[n, 1, part, :] = last
            return cols

        wcp[n] = lax.fori_loop(0, 4, one, jnp.zeros((CHUNK, 128), F32))
        for copy in wave_halo[n]:
            copy.start()

    def advect(n, dst):
        for copy in wave_halo[n]:
            copy.wait()
        cols = jnp.where(
            lane_c % 2 == 0,
            pltpu.roll(wcr[n, 0], 96, 1) * has_left,
            pltpu.roll(wcr[n, 1], 30, 1) * has_right,
        )
        flow_x = jnp.where(seg == 0, has_up, 1.0)
        flow_y = jnp.where(pos == 0, has_left, 1.0)

        def one(k, carry):
            part = pl.ds(pl.multiple_of(CHUNK * k, 8), CHUNK)
            above = wrr[n, 0, part, :] * has_up
            below = wrr[n, 1, part, :] * has_down
            for q in range(4):
                rows = pl.ds(pl.multiple_of(288 * q + CHUNK * k, 8), CHUNK)
                group = 4 * q + k
                g = g_v[rows, :]
                cx, cy = cx_v[rows, :], cy_v[rows, :]
                edge = pltpu.roll(cols, (128 - 2 * group) % 128, 1)
                g_down = jnp.where(
                    seg == 3, pltpu.roll(below, (96 - 32 * q) % 128, 1), pltpu.roll(g, 96, 1)
                )
                g_up = jnp.where(
                    seg == 0, pltpu.roll(above, (128 - 32 * q) % 128, 1), pltpu.roll(g, 32, 1)
                )
                g_right = jnp.where(pos == 31, edge, pltpu.roll(g, 127, 1))
                g_left = jnp.where(pos == 0, edge, pltpu.roll(g, 1, 1))
                px_, nx_ = jnp.maximum(cx, 0.0), jnp.minimum(cx, 0.0)
                py_, ny_ = jnp.maximum(cy, 0.0), jnp.minimum(cy, 0.0)
                out_x = px_ * g + nx_ * g_down
                in_x = flow_x * (px_ * g_up + nx_ * g)
                out_y = py_ * g + ny_ * g_right
                in_y = flow_y * (py_ * g_left + ny_ * g)
                dst[rows, :] = sea_row * (g - (out_x - in_x) - (out_y - in_y))
            return carry

        lax.fori_loop(0, 4, one, 0)

    substep(0, oa_v, ob_v, True)
    grow(0, r2)
    substep(1, ob_v, oa_v, True)
    currents_out(oa_v, s4)
    exchange_all(3, s4, r4)
    advect(0, e_v)
    c_v[...] = e_v[...].astype(BF16)
    drift_out(s3)
    exchange_all(2, s3, r3)
    linear(0, 12)
    grow(1, r4)
    exchange_come(2, r3)
    at_v[...] = arrived(r3).T[0:PLANES] * 0.5
    substep(2, oa_v, ob_v, True)
    advect(1, eout_v)
    substep(3, ob_v, oout_v, False)
    for n, src in enumerate((s1, s2, s3, s4)):
        exchange_sent(n, src)


def step(spectrum, weights, drift, courant, tile, cell, land, vel, oland):
    near_by = pl.BlockSpec(memory_space=pltpu.VMEM)
    far = pl.BlockSpec(memory_space=pltpu.HBM)
    v = pltpu.VMEM
    d = pltpu.SemaphoreType.DMA
    block = v((DEVS, 2, 128), F32)
    args = [
        pltpu.with_memory_space_constraint(x, pltpu.HBM)
        for x in (
            spectrum, weights, drift, courant,
            tile.reshape(1, PTS), cell.reshape(1, PTS), land.reshape(1, PTS),
            vel.reshape(PLANES, 128, 128), oland,
        )
    ]
    e, o = pl.pallas_call(
        kernel,
        out_shape=(
            jax.ShapeDtypeStruct((BINS, PTS), F32),
            jax.ShapeDtypeStruct((PLANES, 128, 128), F32),
        ),
        in_specs=[far] * 9,
        out_specs=(near_by, near_by),
        scratch_shapes=[
            v((BINS, 128), F32), v((BINS, 128), BF16), v((BINS, 128), F32),
            v((4, BINS, 128), F32), v((4, BINS, BINS), BF16), v((PLANES, BINS), BF16),
            v((BINS, 128), F32), v((BINS, 128), F32),
            v((PLANES, PAD, 128), F32), v((PLANES, PAD, 128), F32),
            v((PLANES, 128, 128), F32), v((128, 128), F32), v((128, 128), jnp.int32), v((256, 128), BF16),
            v((2, 128, 128), BF16), v((128, 256), BF16), v((256, 128), BF16),
            v((256, 128), BF16), v((PLANES, 256), F32),
            v((2, BINS), F32), v((1, PTS), jnp.int32), v((1, PTS), jnp.int32), v((1, PTS), jnp.int32),
            block, block, block, block, block, block, block, block,
            v((4, 2, PLANES, 128), F32), v((4, 2, PLANES, 128), F32),
            v((4, 128, 128), F32), v((4, 2, 128, 128), F32), v((128, 128), F32),
            v((2, 2, 288, 128), F32), v((2, 2, 288, 128), F32),
            v((2, CHUNK, 128), F32), v((2, 2, CHUNK, 128), F32),
            d((8,)), d((4,)), d((4,)), d((4,)),
            d((4, 4)), d((4, 4)), d((2, 4)), d((2, 4)),
        ],
        name="coupled",
        compiler_params=pltpu.CompilerParams(
            collective_id=0, has_side_effects=True, vmem_limit_bytes=42 * 1024 * 1024
        ),
    )(*args)
    return e, o.reshape(2, LEV, 128, 128)


def solution(mesh):
    ocean = P(None, None, ("mp", "gx"), "gy")
    return jax.shard_map(
        step,
        mesh=mesh,
        in_specs=(
            P(None, ALL), P(), P(), P(), P(ALL, None), P(ALL), P(ALL),
            ocean, P(("mp", "gx"), "gy"),
        ),
        out_specs=(P(None, ALL), ocean),
        check_vma=False,
    )
```
